256 devices in a mesh: pages: 32 (over x, y, core), mlp: 8 (over z).
Axes of the slice: x: 4, y: 4, z: 8, core: 2. Of those that a mesh axis runs over, the one named last changes fastest.
Arguments:
- embeddings: bfloat16 [8192, 1024], P('pages', 'mlp'), may hold values from -6 to 6
- w_query: bfloat16 [1024, 1024], P(None, 'mlp'), may hold values from -0.1875 to 0.1875
- w_key: bfloat16 [1024, 1024], P(None, 'mlp'), may hold values from -0.1875 to 0.1875
- w_value: bfloat16 [1024, 1024], P(None, 'mlp'), may hold values from -0.1875 to 0.1875
- w_global_query: bfloat16 [1024, 1024], P(None, 'mlp'), may hold values from -0.1875 to 0.1875
- w_out: bfloat16 [1024, 1024], P('mlp'), may hold values from -0.75 to 0.75
- w_up: bfloat16 [1024, 4096], P(None, 'mlp'), may hold values from -0.1875 to 0.1875
- w_down: bfloat16 [4096, 1024], P('mlp'), may hold values from -0.09375 to 0.09375
- norm1_gain: float32 [1024], replicated, may hold values from 0.1 to 1.9
- norm1_bias: float32 [1024], replicated, may hold values from -3 to 3
- norm2_gain: float32 [1024], replicated, may hold values from 0.1 to 1.9
- norm2_bias: float32 [1024], replicated, may hold values from -3 to 3
- cache_keys: bfloat16 [2048, 128, 1024], P('pages', None, 'mlp'), may hold values from -48 to 48
- cache_values: bfloat16 [2048, 128, 1024], P('pages', None, 'mlp'), may hold values from -6 to 6
- lengths: int32 [32], replicated, may hold values from 1 to 8192, as said below
- page_table: int32 [32, 64], replicated, may hold values from -1 to 2047, as said below
- accept: int32 [2, 8192], P(None, 'pages'), may hold values 0 or 1
Outputs:
- refined: bfloat16 [8192, 1024], P('pages', 'mlp')
The draws below stay inside these ranges and needn't reach their ends.
Inputs may be any that keep to these rules, and one draw needn't show every extreme that they name: `lengths`: one request has exactly 8192 cached tokens. page_table[r, j] is the global slot (holder index times 64 plus local slot) of page j of request r for j < ceil(lengths[r] / 128), and -1 for later j; no slot is named twice; the pages of one request lie on at most 8 page holders, at most 8 on one holder, and the longest request has exactly 8 on each of 8 holders.
All inputs are finite; a program needn't handle non-finite values. No bound on the sum of `accept` on one device may be relied on, other than what follows from the above.
Results may differ from the reference program's by a relative error of at most 0.01.
The reference program's roundings to bfloat16 on the way count: a program that leaves them out, or rounds other values in their place, can miss the bound.
Values may be sent and summed in bfloat16 or wider, within the bound.
No kernel may reach another device: no remote copies, remote signals or barrier semaphores. Data moves between devices by JAX's collectives and lax.ppermute only.
A program may use at most 128 MiB of HBM per device.

```python
import jax
import jax.numpy as jnp
from jax import lax

D = 1024
H = 16
HD = 64
FF = 4096
BLK = 256
PAGE = 128
R_DEV = 1
SPAN = 8
HOLD = 8
REQS = 32
TOKENS = 8192
MAXP = 64
LMAX = 8192
SLOT_DEV = 64
SLOTS = 2048


def lengths_and_table(key):
    base_key = jax.random.fold_in(key, 7)
    holders = REQS // R_DEV
    drawn_len = jax.random.randint(jax.random.fold_in(base_key, 1), (REQS,), 1, LMAX + 1)
    longest = jax.random.randint(jax.random.fold_in(base_key, 2), (), 0, REQS)
    lengths = jnp.where(jnp.arange(REQS) == longest, LMAX, drawn_len).astype(jnp.int32)
    needed = (lengths + PAGE - 1) // PAGE
    priority = jax.random.permutation(jax.random.fold_in(base_key, 3), holders)
    request_ids = jnp.arange(REQS)
    span_index = jnp.arange(SPAN)
    holder_of = priority[(request_ids[:, None] + span_index[None, :]) % holders]
    counts = jnp.clip(needed[:, None] - span_index[None, :] * HOLD, 0, HOLD)
    holder_ids = jnp.arange(holders)
    on_holder = jnp.sum(jnp.where(holder_of[:, :, None] == holder_ids[None, None, :], counts[:, :, None], 0), axis=1)
    offsets = jnp.cumsum(on_holder, axis=0) - on_holder
    page_index = jnp.arange(MAXP)
    group_index = page_index // HOLD
    page_holder = holder_of[:, group_index]
    local_slot = jnp.take_along_axis(offsets, page_holder, axis=1) + (page_index % HOLD)[None, :]
    subkeys = jax.random.split(jax.random.fold_in(base_key, 4), holders)
    shuffles = jax.vmap(lambda subkey: jax.random.permutation(subkey, SLOT_DEV))(subkeys)
    placed = page_holder * SLOT_DEV + shuffles[page_holder, jnp.minimum(local_slot, SLOT_DEV - 1)]
    page_table = jnp.where(page_index[None, :] < needed[:, None], placed, -1)
    return (lengths, page_table.astype(jnp.int32))


def draw_lengths(key, part):
    return lengths_and_table(key)[0]


def draw_page_table(key, part):
    return lengths_and_table(key)[1]


def draw_cache_keys(key, part):
    shape_all = (SLOTS, PAGE, D)
    result = jnp.clip(1.5 * jax.random.normal(jax.random.fold_in(key, 4), shape_all, jnp.float32), -9.0, 9.0)
    return result.astype(jnp.bfloat16)


def touch_ends(array, stream_key, least, high):
    dims = array.shape
    spot = [jax.random.randint(jax.random.fold_in(stream_key, axis), (), 0, dims[axis]) for axis in range(len(dims))]
    array = array.at[tuple(spot)].set(least)
    longest = dims.index(max(dims))
    spot[longest] = (spot[longest] + 1) % dims[longest]
    return array.at[tuple(spot)].set(high)


def block_scale(own_key, shape, cuts, smallest, high):
    def one(dim, shards_of):
        draws = jax.random.uniform(jax.random.fold_in(jax.random.fold_in(own_key, 6), dim), (shards_of,), jnp.float32, smallest / len(cuts), high / len(cuts))
        return jnp.repeat(jnp.exp(draws), shape[dim] // shards_of).reshape((-1,) + (1,) * (len(shape) - dim - 1))

    level = one(*cuts[0])
    for cut in cuts[1:]:
        level = level * one(*cut)
    return level


def normal_values(key, extent, spread, limit, pieces=(), kind=jnp.bfloat16):
    loudness = block_scale(key, extent, pieces, -0.22, 0.18) if pieces else 1.0
    entries = jax.random.normal(key, extent, jnp.float32) * spread * loudness
    return jnp.minimum(jnp.maximum(entries, -limit), limit).astype(kind)


def setup_inputs(seed: int = 0) -> dict:
    arg_keys = jax.random.split(jax.random.key(seed), 18)
    embeddings = normal_values(arg_keys[0], (TOKENS, D), 1.0, 6.0, ((0, 32), (1, 8)))
    w_query = normal_values(arg_keys[1], (D, D), D ** -0.5, 0.1875, ((1, 8),))
    w_key = normal_values(arg_keys[2], (D, D), D ** -0.5, 0.1875, ((1, 8),))
    w_value = normal_values(arg_keys[3], (D, D), D ** -0.5, 0.1875, ((1, 8),))
    w_global_query = normal_values(arg_keys[4], (D, D), D ** -0.5, 0.1875, ((1, 8),))
    w_out = normal_values(arg_keys[5], (D, D), HD ** -0.5, 0.75, ((0, 8),))
    w_up = normal_values(arg_keys[6], (D, FF), D ** -0.5, 0.1875, ((1, 8),))
    w_down = normal_values(arg_keys[7], (FF, D), FF ** -0.5, 0.09375, ((0, 8),))
    norm1_gain = jnp.clip(1.0 + 0.18 * jax.random.normal(arg_keys[8], (D,), jnp.float32), 0.1, 1.9)
    norm1_bias = normal_values(arg_keys[9], (D,), 0.5, 3.0, (), jnp.float32)
    norm2_gain = jnp.clip(1.0 + 0.18 * jax.random.normal(arg_keys[10], (D,), jnp.float32), 0.1, 1.9)
    norm2_bias = normal_values(arg_keys[11], (D,), 0.5, 3.0, (), jnp.float32)
    cache_keys = draw_cache_keys(jax.random.fold_in(arg_keys[17], 71), 0)
    cache_values = normal_values(arg_keys[13], (SLOTS, PAGE, D), 1.0, 6.0, ((0, 32), (2, 8)))
    lengths = draw_lengths(jax.random.fold_in(arg_keys[17], 71), 0)
    page_table = draw_page_table(jax.random.fold_in(arg_keys[17], 71), 0)
    accept = touch_ends((jax.random.randint(arg_keys[16], (2, TOKENS), 0, 2) < 1).astype(jnp.int32), jax.random.fold_in(arg_keys[16], 1), 0, 1)
    return dict(embeddings=embeddings, w_query=w_query, w_key=w_key, w_value=w_value, w_global_query=w_global_query, w_out=w_out, w_up=w_up, w_down=w_down, norm1_gain=norm1_gain, norm1_bias=norm1_bias, norm2_gain=norm2_gain, norm2_bias=norm2_bias, cache_keys=cache_keys, cache_values=cache_values, lengths=lengths, page_table=page_table, accept=accept)


neg_big = -1e+30
eps_norm = 1e-05

def layer_norm(totals, gain, bias):
    row_mean = lax.optimization_barrier(jnp.mean(totals, axis=-1, keepdims=True))
    square = lax.optimization_barrier(jnp.mean(totals * totals, axis=-1, keepdims=True))
    inverse = lax.rsqrt(square - row_mean * row_mean + eps_norm)
    return ((totals - row_mean) * inverse * gain + bias).astype(jnp.bfloat16)

def partial_softmax(queries, key_rows, value_rows, usable):
    scores = jnp.einsum('qhd,khd->hqk', queries.astype(jnp.float32), key_rows.astype(jnp.float32)) * HD ** (-0.5)
    masking = usable[None, None, :]
    row_peak = lax.optimization_barrier(jnp.max(jnp.where(masking, scores, neg_big), axis=-1))
    weights = jnp.where(masking, jnp.exp(scores - row_peak[..., None]), 0.0)
    totals = lax.optimization_barrier(jnp.sum(weights, axis=-1))
    rounded = lax.optimization_barrier(weights.astype(jnp.bfloat16)).astype(jnp.float32)
    weighted = jnp.einsum('hqk,khd->qhd', rounded, value_rows.astype(jnp.float32))
    return (weighted, row_peak.T, totals.T)

def merge_parts(first_part, second_part):
    row_peak = jnp.maximum(first_part[1], second_part[1])
    first_factor = jnp.exp(first_part[1] - row_peak)
    second_factor = jnp.exp(second_part[1] - row_peak)
    weighted = first_part[0] * first_factor[..., None] + second_part[0] * second_factor[..., None]
    return (weighted, row_peak, first_part[2] * first_factor + second_part[2] * second_factor)

def cache_pass(queries, table_row, length, cache_keys, cache_values):
    initial = (jnp.zeros((BLK, H, HD), jnp.float32), jnp.full((BLK, H), neg_big, jnp.float32), jnp.zeros((BLK, H), jnp.float32))
    page_total = (length + PAGE - 1) // PAGE

    def page_step(page_index, state_now):
        slot_index = table_row[page_index].astype(jnp.int32)
        key_rows = lax.dynamic_index_in_dim(cache_keys, slot_index, 0, keepdims=False).reshape(PAGE, H, HD)
        value_rows = lax.dynamic_index_in_dim(cache_values, slot_index, 0, keepdims=False).reshape(PAGE, H, HD)
        usable = page_index * PAGE + jnp.arange(PAGE, dtype=jnp.int32) < length
        return merge_parts(state_now, partial_softmax(queries, key_rows, value_rows, usable))
    return lax.fori_loop(0, page_total, page_step, initial)

def one_layer(inputs, w_query, w_key, w_value, w_global_query, w_out, w_up, w_down, norm1_gain, norm1_bias, norm2_gain, norm2_bias, cache_keys, cache_values, lengths, page_table):

    def project(matrix):
        return jnp.dot(inputs, matrix, preferred_element_type=jnp.float32).astype(jnp.bfloat16).reshape(REQS, BLK, H, HD)
    queries = project(w_query)
    key_rows = project(w_key)
    value_rows = project(w_value)
    global_rows = project(w_global_query)

    def request_pass(request_data):
        own_queries, own_keys, own_values, own_global, table_row, length = request_data
        block_part = partial_softmax(own_queries, own_keys, own_values, jnp.ones((BLK,), jnp.bool_))
        cache_part = cache_pass(own_global, table_row, length, cache_keys, cache_values)
        merged = merge_parts(cache_part, block_part)
        return (merged[0] / merged[2][..., None]).astype(jnp.bfloat16)
    attention = lax.map(request_pass, (queries, key_rows, value_rows, global_rows, page_table, lengths)).reshape(TOKENS, D)
    attn_out = jnp.dot(attention, w_out, preferred_element_type=jnp.float32)
    hidden = layer_norm(inputs.astype(jnp.float32) + attn_out, norm1_gain, norm1_bias)
    up_proj = jnp.dot(hidden, w_up, preferred_element_type=jnp.float32)
    active = jax.nn.gelu(up_proj, approximate=False).astype(jnp.bfloat16)
    down_proj = jnp.dot(active, w_down, preferred_element_type=jnp.float32)
    return layer_norm(hidden.astype(jnp.float32) + down_proj, norm2_gain, norm2_bias)

def reference(embeddings, w_query, w_key, w_value, w_global_query, w_out, w_up, w_down, norm1_gain, norm1_bias, norm2_gain, norm2_bias, cache_keys, cache_values, lengths, page_table, accept):
    shared = (w_query, w_key, w_value, w_global_query, w_out, w_up, w_down, norm1_gain, norm1_bias, norm2_gain, norm2_bias, cache_keys, cache_values, lengths, page_table)
    first_out = one_layer(embeddings, *shared)
    middle = jnp.where(accept[0][:, None] != 0, first_out, embeddings)
    second_out = one_layer(middle, *shared)
    return jnp.where(accept[1][:, None] != 0, second_out, middle)
```

```python
import functools

import jax
import jax.numpy as jnp
from jax import lax
from jax.experimental import pallas as pl
from jax.experimental.pallas import tpu as pltpu
from jax.sharding import PartitionSpec as P

HD = 64
BLK = 256
PAGE = 128
EPS = 1e-05
NEG = -1e30
CAP = 2
KEY_BLOCK = 1024
F32 = jnp.float32
BF16 = jnp.bfloat16
VMEM = pl.BlockSpec(memory_space=pltpu.VMEM)
ANY = pl.BlockSpec(memory_space=pl.ANY)
SMEM = pl.BlockSpec(memory_space=pltpu.SMEM)


def routing(page_table, me, holders, slots, hold):
    requests, pages = page_table.shape
    i32 = jnp.int32
    holder_of = jnp.where(page_table >= 0, page_table // slots, -1)
    ids = jnp.arange(holders, dtype=i32)
    page_ids = jnp.arange(pages, dtype=i32)
    on = holder_of[:, None, :] == ids[None, :, None]
    first = jnp.min(jnp.where(on, page_ids[None, None, :], pages), axis=2)
    count = jnp.sum(on.astype(i32), axis=2)
    rank = jnp.sum((first[:, None, :] < first[:, :, None]).astype(i32), axis=2)
    groups = holders // hold
    request_ids = jnp.arange(requests, dtype=i32)
    earlier = request_ids[None, :] < request_ids[:, None]

    def before(sent):
        return jnp.sum((earlier[:, :, None] & sent[None, :, :]).astype(i32), axis=1)

    my_rank = lax.dynamic_slice_in_dim(rank, me, 1, 1)
    my_count = lax.dynamic_slice_in_dim(count, me, 1, 1)
    to = (my_rank % groups == ids[None, :] // hold) & (my_count > ids[None, :] % hold)
    to_turn = before(to)
    mine = holder_of == me
    nth = jnp.sum(
        ((page_ids[None, :, None] > page_ids[None, None, :]) & mine[:, None, :]).astype(i32), axis=2
    )
    local = page_table % slots
    hit = mine[:, None, :] & (nth[:, None, :] == (ids % hold)[None, :, None])
    source = jnp.sum(jnp.where(hit, local[:, None, :], 0), axis=2)

    def send_table(turn):
        want = turn * CAP + jnp.arange(CAP, dtype=i32)
        chosen = to[:, :, None] & (to_turn[:, :, None] == want[None, None, :])
        return jnp.sum(jnp.where(chosen, source[:, :, None], 0), axis=0).reshape(-1)

    places = pages // holders
    came = (rank % groups == me // hold) & (count > me % hold)
    came_turn = before(came)

    def pass_table(turn):
        place = rank // groups
        chosen = (
            came[:, :, None]
            & (place[:, :, None] == jnp.arange(places, dtype=i32)[None, None, :])
            & (came_turn // CAP == turn)[:, :, None]
        )
        origin = ids[None, :] * CAP + came_turn % CAP + 1
        return (jnp.sum(jnp.where(chosen, origin[:, :, None], 0), axis=1) - 1).reshape(-1)

    all_to = (rank[:, :, None] % groups == ids[None, None, :] // hold) & (
        count[:, :, None] > ids[None, None, :] % hold
    )
    rounds = (jnp.max(jnp.sum(all_to.astype(i32), axis=0)) + CAP - 1) // CAP

    own_holder = lax.dynamic_slice_in_dim(holder_of, me, 1, 0)[0]
    own_rank = lax.dynamic_slice_in_dim(rank, me, 1, 0)[0]
    page_rank = jnp.sum(
        jnp.where(own_holder[:, None] == ids[None, :], own_rank[None, :], 0), axis=1
    )
    page_nth = jnp.sum(
        (
            (page_ids[None, :] < page_ids[:, None])
            & (own_holder[None, :] == own_holder[:, None])
        ).astype(i32),
        axis=1,
    )
    unit = page_rank * hold + page_nth
    found = jnp.where(own_holder >= 0, (unit % holders) * places + unit // holders, 0)
    return send_table, pass_table, rounds, found


def pack_kernel(table, keys, values, packed, sem):
    total = packed.shape[0]

    def start(i, carry):
        slot = table[i]
        pltpu.make_async_copy(keys.at[slot], packed.at[i, 0], sem).start()
        pltpu.make_async_copy(values.at[slot], packed.at[i, 1], sem).start()
        return carry

    lax.fori_loop(0, total, start, 0)
    pltpu.make_async_copy(packed, packed, sem).wait()


def pack_pages(table, keys, values):
    shape = (table.shape[0], 2) + keys.shape[1:]
    return pl.pallas_call(
        pack_kernel,
        out_shape=jax.ShapeDtypeStruct(shape, BF16),
        in_specs=[SMEM, ANY, ANY],
        out_specs=ANY,
        scratch_shapes=[pltpu.SemaphoreType.DMA],
        name="pack_pages",
    )(table, keys, values)


def repack_kernel(table, got, packed, sem):
    total = packed.shape[0]

    def start(i, carry):
        pltpu.make_async_copy(got.at[jnp.maximum(table[i], 0)], packed.at[i], sem).start()
        return carry

    lax.fori_loop(0, total, start, 0)
    pltpu.make_async_copy(packed, packed, sem).wait()


def repack_pages(table, got):
    return pl.pallas_call(
        repack_kernel,
        out_shape=jax.ShapeDtypeStruct(got.shape, BF16),
        in_specs=[SMEM, ANY],
        out_specs=ANY,
        scratch_shapes=[pltpu.SemaphoreType.DMA],
        name="repack_pages",
    )(table, got)


def exchange(pages):
    holders = lax.axis_size("pages")
    shape = pages.shape
    sent = lax.all_to_all(
        pages.reshape((holders, shape[0] // holders) + shape[1:]), "pages", 0, 0, tiled=True
    )
    return sent.reshape(shape)


def pages_to_owners(page_table, keys, values):
    holders = lax.axis_size("pages")
    me = lax.axis_index("pages")
    hold = 8
    send_table, pass_table, rounds, found = routing(page_table, me, holders, keys.shape[0], hold)
    first = exchange(pack_pages(send_table(0), keys, values))
    middle = repack_pages(pass_table(0), first)

    def further(turn, middle):
        got = exchange(pack_pages(send_table(turn), keys, values))
        table = pass_table(turn)
        return jnp.where((table >= 0)[:, None, None, None], repack_pages(table, got), middle)

    middle = lax.fori_loop(1, rounds, further, middle)
    return exchange(middle), found


def two_heads(rows):
    lane = lax.broadcasted_iota(jnp.int32, rows.shape, 1)
    low = jnp.where(lane < HD, rows, 0.0)
    high = jnp.where(lane < HD, 0.0, rows)
    return jnp.concatenate([low, high], axis=0).astype(BF16)


def attention_kernel(
    found, length, x_ref, wq, wk, wv, wg, pages, out, x_all, key_buf, value_buf, acc, peak, ksem, vsem
):
    per_block = KEY_BLOCK // PAGE
    shards = x_ref.shape[0]
    width = x_ref.shape[2]
    limit = length[0]
    blocks = (limit + KEY_BLOCK - 1) // KEY_BLOCK

    def fetch(block, carry):
        for i in range(per_block):
            page = block * per_block + i
            place = found[page]
            rows = pl.ds(pl.multiple_of(page * PAGE, PAGE), PAGE)
            pltpu.make_async_copy(pages.at[place, 0], key_buf.at[rows], ksem.at[block]).start()
            pltpu.make_async_copy(pages.at[place, 1], value_buf.at[rows], vsem.at[block]).start()
        return carry

    lax.fori_loop(0, blocks, fetch, 0)
    for i in range(shards):
        x_all[:, i * width : (i + 1) * width] = x_ref[i]
    x = x_all[...]

    def project(matrix):
        return jnp.dot(x, matrix[...], preferred_element_type=F32).astype(BF16)

    scale = HD ** (-0.5)
    queries = two_heads(project(wq).astype(F32) * scale)
    global_rows = two_heads(project(wg).astype(F32) * scale)
    key_rows = project(wk)
    value_rows = project(wv)

    def scores_of(left, keys):
        return lax.dot_general(left, keys, (((1,), (1,)), ((), ())), preferred_element_type=F32)

    def weigh(weights, values):
        ones = jnp.ones(values.shape, BF16)
        return jnp.dot(
            weights, jnp.concatenate([values, ones], axis=1), preferred_element_type=F32
        )

    scores = scores_of(queries, key_rows)
    top = jnp.max(scores, axis=1, keepdims=True)
    weights = jnp.exp(scores - top).astype(BF16)
    acc[...] = weigh(weights, value_rows)
    peak[...] = jnp.broadcast_to(top, peak.shape)

    def step(block, masked):
        rows = pl.ds(pl.multiple_of(block * KEY_BLOCK, KEY_BLOCK), KEY_BLOCK)
        pltpu.make_async_copy(key_buf.at[rows], key_buf.at[rows], ksem.at[block]).wait()
        pltpu.make_async_copy(value_buf.at[rows], value_buf.at[rows], vsem.at[block]).wait()
        scores = scores_of(global_rows, key_buf[rows, :])
        if masked:
            position = block * KEY_BLOCK + lax.broadcasted_iota(jnp.int32, scores.shape, 1)
            scores = jnp.where(position < limit, scores, NEG)
        old = peak[:, :1]
        new = jnp.maximum(old, jnp.max(scores, axis=1, keepdims=True))
        weights = jnp.exp(scores - new).astype(BF16)
        keep = jnp.exp(old - new)
        acc[...] = acc[...] * keep + weigh(weights, value_buf[rows, :])
        peak[...] = jnp.broadcast_to(new, peak.shape)

    def whole(block, carry):
        step(block, False)
        return carry

    lax.fori_loop(0, blocks - 1, whole, 0)
    step(blocks - 1, True)
    rows = x_ref.shape[1]
    total = acc[...]
    ratio = total[:, :width] / total[:, width:]
    lane = lax.broadcasted_iota(jnp.int32, (rows, width), 1)
    result = jnp.where(lane < HD, ratio[:rows], ratio[rows:]).astype(BF16)
    for i in range(shards):
        out[i] = result


def attend(found, length, x_parts, wq, wk, wv, wg, pages):
    shards, rows, width = x_parts.shape
    longest = found.shape[0] * PAGE
    return pl.pallas_call(
        attention_kernel,
        out_shape=jax.ShapeDtypeStruct(x_parts.shape, BF16),
        in_specs=[SMEM, SMEM, VMEM, VMEM, VMEM, VMEM, VMEM, ANY],
        out_specs=VMEM,
        scratch_shapes=[
            pltpu.VMEM((rows, shards * width), BF16),
            pltpu.VMEM((longest, width), BF16),
            pltpu.VMEM((longest, width), BF16),
            pltpu.VMEM((2 * rows, 2 * width), F32),
            pltpu.VMEM((2 * rows, 128), F32),
            pltpu.SemaphoreType.DMA((longest // KEY_BLOCK,)),
            pltpu.SemaphoreType.DMA((longest // KEY_BLOCK,)),
        ],
        compiler_params=pltpu.CompilerParams(vmem_limit_bytes=48 << 20),
        name="attention",
    )(found, length, x_parts, wq, wk, wv, wg, pages)


def normalize(total, gain, bias, width):
    mean = jnp.sum(total, axis=1, keepdims=True) * (1.0 / width)
    square = jnp.sum(total * total, axis=1, keepdims=True) * (1.0 / width)
    inverse = lax.rsqrt(square - mean * mean + EPS)
    return ((total - mean) * inverse * gain + bias).astype(BF16)


def ffn_kernel(
    att, x_ref, accept, w_out, up_a, up_b, down_a, down_b, g1, b1, g2, b2, out, wide, hidden, acc
):
    step = pl.program_id(0)
    shards, rows, width = x_ref.shape
    full = shards * width

    @pl.when(step == 0)
    def _():
        for i in range(shards):
            wide[:, i * width : (i + 1) * width] = att[i]
        total = jnp.dot(wide[...], w_out[...], preferred_element_type=F32)
        for i in range(shards):
            wide[:, i * width : (i + 1) * width] = x_ref[i]
        total = total + wide[...].astype(F32)
        hidden[...] = normalize(total, g1[...], b1[...], full)
        acc[...] = hidden[...].astype(F32)

    h = hidden[...]
    for up, down in ((up_a, down_a), (up_b, down_b)):
        raised = jnp.dot(h, up[0], preferred_element_type=F32)
        active = (0.5 * raised * (1.0 + lax.erf(raised * (0.5**0.5)))).astype(BF16)
        acc[...] += jnp.dot(active, down[0], preferred_element_type=F32)

    @pl.when(step == pl.num_programs(0) - 1)
    def _():
        result = normalize(acc[...], g2[...], b2[...], full)
        chosen = accept[...] != 0
        for i in range(shards):
            out[i] = jnp.where(chosen, result[:, i * width : (i + 1) * width], x_ref[i])


def feed_forward(att, x_parts, accept, w_out, up, down, g1, b1, g2, b2):
    shards, rows, width = x_parts.shape
    full = shards * width

    def fixed(shape):
        return pl.BlockSpec(shape, lambda i: (0,) * len(shape), pipeline_mode=pl.Buffered(1))

    def part(array):
        return pl.BlockSpec((1,) + array.shape[1:], lambda i: (i, 0, 0))

    return pl.pallas_call(
        ffn_kernel,
        grid=(up[0].shape[0],),
        out_shape=jax.ShapeDtypeStruct(x_parts.shape, BF16),
        in_specs=[
            fixed(x_parts.shape),
            fixed(x_parts.shape),
            fixed((rows, 1)),
            fixed(w_out.shape),
            part(up[0]),
            part(up[1]),
            part(down[0]),
            part(down[1]),
        ]
        + [fixed((1, full))] * 4,
        out_specs=pl.BlockSpec(x_parts.shape, lambda i: (0, 0, 0)),
        scratch_shapes=[
            pltpu.VMEM((rows, full), BF16),
            pltpu.VMEM((rows, full), BF16),
            pltpu.VMEM((rows, full), F32),
        ],
        compiler_params=pltpu.CompilerParams(
            dimension_semantics=("arbitrary",), vmem_limit_bytes=48 << 20
        ),
        name="feed_forward",
    )(att, x_parts, accept, w_out, up[0], up[1], down[0], down[1], g1, b1, g2, b2)


def to_all(copies):
    return lax.all_to_all(copies, "mlp", 0, 0, tiled=True)


def core_pair():
    return [(i, i ^ 1) for i in range(lax.axis_size("pages"))]


def per_device(
    embeddings,
    w_query,
    w_key,
    w_value,
    w_global_query,
    w_out,
    w_up,
    w_down,
    norm1_gain,
    norm1_bias,
    norm2_gain,
    norm2_bias,
    cache_keys,
    cache_values,
    lengths,
    page_table,
    accept,
):
    shards = lax.axis_size("mlp")
    me = lax.axis_index("pages")
    shard = lax.axis_index("mlp")
    rows, width = embeddings.shape
    pages, found = pages_to_owners(page_table, cache_keys, cache_values)
    length = lax.dynamic_slice_in_dim(lengths, me, 1, 0)

    core = me % 2
    half = w_up.shape[1] // 2
    up_half = lax.dynamic_slice_in_dim(w_up, core * half, half, 1)
    down_half = lax.dynamic_slice_in_dim(w_down, core * half, half, 0)
    w_out_all = lax.all_gather(w_out, "mlp", axis=0, tiled=True)
    up_mine = lax.all_gather(up_half, "mlp", axis=0)
    down_mine = lax.all_gather(down_half, "mlp", axis=0)
    up_other = lax.ppermute(up_mine, "pages", core_pair())
    down_other = lax.ppermute(down_mine, "pages", core_pair())
    norms = [v.reshape(1, -1) for v in (norm1_gain, norm1_bias, norm2_gain, norm2_bias)]

    x_parts = to_all(jnp.broadcast_to(embeddings[None], (shards, rows, width)))
    for pass_index in range(2):
        attention = attend(
            found, length, x_parts, w_query, w_key, w_value, w_global_query, pages
        )
        x_parts = feed_forward(
            to_all(attention),
            x_parts,
            accept[pass_index].reshape(rows, 1),
            w_out_all,
            (up_mine, up_other),
            (down_mine, down_other),
            *norms,
        )
    return lax.dynamic_index_in_dim(x_parts, shard, 0, keepdims=False)


def solution(mesh):
    return jax.shard_map(
        per_device,
        mesh=mesh,
        in_specs=(
            P("pages", "mlp"),
            P(None, "mlp"),
            P(None, "mlp"),
            P(None, "mlp"),
            P(None, "mlp"),
            P("mlp", None),
            P(None, "mlp"),
            P("mlp", None),
            P(),
            P(),
            P(),
            P(),
            P("pages", None, "mlp"),
            P("pages", None, "mlp"),
            P(),
            P(),
            P(None, "pages"),
        ),
        out_specs=P("pages", "mlp"),
        check_vma=False,
    )
```

```python
import functools

import jax
import jax.numpy as jnp
from jax import lax
from jax.experimental import pallas as pl
from jax.experimental.pallas import tpu as pltpu
from jax.sharding import PartitionSpec as P

HD = 64
BLK = 256
PAGE = 128
EPS = 1e-05
NEG = -1e30
CAP = 2
KEY_BLOCK = 1024
GROUP = 8
F32 = jnp.float32
BF16 = jnp.bfloat16
VMEM = pl.BlockSpec(memory_space=pltpu.VMEM)
ANY = pl.BlockSpec(memory_space=pl.ANY)
SMEM = pl.BlockSpec(memory_space=pltpu.SMEM)


def routing(page_table, me, holders, slots, hold):
    requests, pages = page_table.shape
    i32 = jnp.int32
    holder_of = jnp.where(page_table >= 0, page_table // slots, -1)
    ids = jnp.arange(holders, dtype=i32)
    page_ids = jnp.arange(pages, dtype=i32)
    on = holder_of[:, None, :] == ids[None, :, None]
    first = jnp.min(jnp.where(on, page_ids[None, None, :], pages), axis=2)
    count = jnp.sum(on.astype(i32), axis=2)
    rank = jnp.sum((first[:, None, :] < first[:, :, None]).astype(i32), axis=2)
    groups = holders // hold
    request_ids = jnp.arange(requests, dtype=i32)
    earlier = request_ids[None, :] < request_ids[:, None]

    def before(sent):
        return jnp.sum((earlier[:, :, None] & sent[None, :, :]).astype(i32), axis=1)

    my_rank = lax.dynamic_slice_in_dim(rank, me, 1, 1)
    my_count = lax.dynamic_slice_in_dim(count, me, 1, 1)
    to = (my_rank % groups == ids[None, :] // hold) & (my_count > ids[None, :] % hold)
    to_turn = before(to)
    mine = holder_of == me
    nth = jnp.sum(
        ((page_ids[None, :, None] > page_ids[None, None, :]) & mine[:, None, :]).astype(i32), axis=2
    )
    local = page_table % slots
    hit = mine[:, None, :] & (nth[:, None, :] == (ids % hold)[None, :, None])
    source = jnp.sum(jnp.where(hit, local[:, None, :], 0), axis=2)

    def send_table(turn):
        want = turn * CAP + jnp.arange(CAP, dtype=i32)
        chosen = to[:, :, None] & (to_turn[:, :, None] == want[None, None, :])
        return jnp.sum(jnp.where(chosen, source[:, :, None], 0), axis=0).reshape(-1)

    places = pages // holders
    came = (rank % groups == me // hold) & (count > me % hold)
    came_turn = before(came)

    def pass_table(turn):
        place = rank // groups
        chosen = (
            came[:, :, None]
            & (place[:, :, None] == jnp.arange(places, dtype=i32)[None, None, :])
            & (came_turn // CAP == turn)[:, :, None]
        )
        origin = ids[None, :] * CAP + came_turn % CAP + 1
        return (jnp.sum(jnp.where(chosen, origin[:, :, None], 0), axis=1) - 1).reshape(-1)

    all_to = (rank[:, :, None] % groups == ids[None, None, :] // hold) & (
        count[:, :, None] > ids[None, None, :] % hold
    )
    rounds = (jnp.max(jnp.sum(all_to.astype(i32), axis=0)) + CAP - 1) // CAP

    own_holder = lax.dynamic_slice_in_dim(holder_of, me, 1, 0)[0]
    own_rank = lax.dynamic_slice_in_dim(rank, me, 1, 0)[0]
    page_rank = jnp.sum(
        jnp.where(own_holder[:, None] == ids[None, :], own_rank[None, :], 0), axis=1
    )
    page_nth = jnp.sum(
        (
            (page_ids[None, :] < page_ids[:, None])
            & (own_holder[None, :] == own_holder[:, None])
        ).astype(i32),
        axis=1,
    )
    unit = page_rank * hold + page_nth
    found = jnp.where(own_holder >= 0, (unit % holders) * places + unit // holders, 0)
    return send_table, pass_table, rounds, found


def staged(total, group, load, stage, packed, got_sem, put_sem):
    for g in range(total // group):
        for i in range(g * group, (g + 1) * group):
            load(i, got_sem.at[g])
    for g in range(total // group):
        part = pl.ds(g * group, group)
        pltpu.make_async_copy(stage.at[part], stage.at[part], got_sem.at[g]).wait()
        pltpu.make_async_copy(stage.at[part], packed.at[part], put_sem).start()
    pltpu.make_async_copy(stage, packed, put_sem).wait()


def pack_kernel(table, keys, values, packed, stage, got_sem, put_sem):
    def load(i, sem):
        slot = table[i]
        pltpu.make_async_copy(keys.at[slot], stage.at[i, 0], sem).start()
        pltpu.make_async_copy(values.at[slot], stage.at[i, 1], sem).start()

    staged(stage.shape[0], GROUP, load, stage, packed, got_sem, put_sem)


def repack_kernel(table, got, packed, stage, got_sem, put_sem):
    def load(i, sem):
        pltpu.make_async_copy(got.at[jnp.maximum(table[i], 0)], stage.at[i], sem).start()

    staged(stage.shape[0], GROUP, load, stage, packed, got_sem, put_sem)


def staged_call(kernel, name, table, page_shape, *arrays):
    shape = (table.shape[0], 2) + page_shape
    return pl.pallas_call(
        kernel,
        out_shape=jax.ShapeDtypeStruct(shape, BF16),
        in_specs=[SMEM] + [ANY] * len(arrays),
        out_specs=ANY,
        scratch_shapes=[
            pltpu.VMEM(shape, BF16),
            pltpu.SemaphoreType.DMA((shape[0] // GROUP,)),
            pltpu.SemaphoreType.DMA,
        ],
        compiler_params=pltpu.CompilerParams(vmem_limit_bytes=16 << 20),
        name=name,
    )(table, *arrays)


def pack_pages(table, keys, values):
    return staged_call(pack_kernel, "pack_pages", table, keys.shape[1:], keys, values)


def repack_pages(table, got):
    return staged_call(repack_kernel, "repack_pages", table, got.shape[2:], got)


def exchange(pages):
    holders = lax.axis_size("pages")
    shape = pages.shape
    sent = lax.all_to_all(
        pages.reshape((holders, shape[0] // holders) + shape[1:]), "pages", 0, 0, tiled=True
    )
    return sent.reshape(shape)


def pages_to_owners(page_table, keys, values):
    holders = lax.axis_size("pages")
    me = lax.axis_index("pages")
    hold = 8
    send_table, pass_table, rounds, found = routing(page_table, me, holders, keys.shape[0], hold)
    first = exchange(pack_pages(send_table(0), keys, values))
    middle = repack_pages(pass_table(0), first)

    def further(turn, middle):
        got = exchange(pack_pages(send_table(turn), keys, values))
        table = pass_table(turn)
        return jnp.where((table >= 0)[:, None, None, None], repack_pages(table, got), middle)

    middle = lax.fori_loop(1, rounds, further, middle)
    return exchange(middle), found


def two_heads(rows):
    lane = lax.broadcasted_iota(jnp.int32, rows.shape, 1)
    low = jnp.where(lane < HD, rows, 0.0)
    high = jnp.where(lane < HD, 0.0, rows)
    return jnp.concatenate([low, high], axis=0).astype(BF16)


def attention_kernel(
    found, length, x_ref, wq, wk, wv, wg, pages, out, x_all, key_buf, value_buf, acc, peak, ksem, vsem
):
    per_block = KEY_BLOCK // PAGE
    shards = x_ref.shape[0]
    width = x_ref.shape[2]
    limit = length[0]
    blocks = (limit + KEY_BLOCK - 1) // KEY_BLOCK

    def fetch(block, carry):
        for i in range(per_block):
            page = block * per_block + i
            place = found[page]
            rows = pl.ds(pl.multiple_of(page * PAGE, PAGE), PAGE)
            pltpu.make_async_copy(pages.at[place, 0], key_buf.at[rows], ksem.at[block]).start()
            pltpu.make_async_copy(pages.at[place, 1], value_buf.at[rows], vsem.at[block]).start()
        return carry

    lax.fori_loop(0, blocks, fetch, 0)
    for i in range(shards):
        x_all[:, i * width : (i + 1) * width] = x_ref[i]
    x = x_all[...]

    def project(matrix):
        return jnp.dot(x, matrix[...], preferred_element_type=F32).astype(BF16)

    scale = HD ** (-0.5)
    queries = two_heads(project(wq).astype(F32) * scale)
    global_rows = two_heads(project(wg).astype(F32) * scale)
    key_rows = project(wk)
    value_rows = project(wv)

    def scores_of(left, keys):
        return lax.dot_general(left, keys, (((1,), (1,)), ((), ())), preferred_element_type=F32)

    def weigh(weights, values):
        ones = jnp.ones(values.shape, BF16)
        return jnp.dot(
            weights, jnp.concatenate([values, ones], axis=1), preferred_element_type=F32
        )

    scores = scores_of(queries, key_rows)
    top = jnp.max(scores, axis=1, keepdims=True)
    weights = jnp.exp(scores - top).astype(BF16)
    acc[...] = weigh(weights, value_rows)
    peak[...] = jnp.broadcast_to(top, peak.shape)

    def step(block, masked):
        rows = pl.ds(pl.multiple_of(block * KEY_BLOCK, KEY_BLOCK), KEY_BLOCK)
        pltpu.make_async_copy(key_buf.at[rows], key_buf.at[rows], ksem.at[block]).wait()
        pltpu.make_async_copy(value_buf.at[rows], value_buf.at[rows], vsem.at[block]).wait()
        scores = scores_of(global_rows, key_buf[rows, :])
        if masked:
            position = block * KEY_BLOCK + lax.broadcasted_iota(jnp.int32, scores.shape, 1)
            scores = jnp.where(position < limit, scores, NEG)
        old = peak[:, :1]
        new = jnp.maximum(old, jnp.max(scores, axis=1, keepdims=True))
        weights = jnp.exp(scores - new).astype(BF16)
        keep = jnp.exp(old - new)
        acc[...] = acc[...] * keep + weigh(weights, value_buf[rows, :])
        peak[...] = jnp.broadcast_to(new, peak.shape)

    def whole(block, carry):
        step(block, False)
        return carry

    lax.fori_loop(0, blocks - 1, whole, 0)
    step(blocks - 1, True)
    rows = x_ref.shape[1]
    total = acc[...]
    ratio = total[:, :width] / total[:, width:]
    lane = lax.broadcasted_iota(jnp.int32, (rows, width), 1)
    result = jnp.where(lane < HD, ratio[:rows], ratio[rows:]).astype(BF16)
    for i in range(shards):
        out[i] = result


def attend(found, length, x_parts, wq, wk, wv, wg, pages):
    shards, rows, width = x_parts.shape
    longest = found.shape[0] * PAGE
    return pl.pallas_call(
        attention_kernel,
        out_shape=jax.ShapeDtypeStruct(x_parts.shape, BF16),
        in_specs=[SMEM, SMEM, VMEM, VMEM, VMEM, VMEM, VMEM, ANY],
        out_specs=VMEM,
        scratch_shapes=[
            pltpu.VMEM((rows, shards * width), BF16),
            pltpu.VMEM((longest, width), BF16),
            pltpu.VMEM((longest, width), BF16),
            pltpu.VMEM((2 * rows, 2 * width), F32),
            pltpu.VMEM((2 * rows, 128), F32),
            pltpu.SemaphoreType.DMA((longest // KEY_BLOCK,)),
            pltpu.SemaphoreType.DMA((longest // KEY_BLOCK,)),
        ],
        compiler_params=pltpu.CompilerParams(vmem_limit_bytes=48 << 20),
        name="attention",
    )(found, length, x_parts, wq, wk, wv, wg, pages)


def normalize(total, gain, bias, width):
    mean = jnp.sum(total, axis=1, keepdims=True) * (1.0 / width)
    square = jnp.sum(total * total, axis=1, keepdims=True) * (1.0 / width)
    inverse = lax.rsqrt(square - mean * mean + EPS)
    return ((total - mean) * inverse * gain + bias).astype(BF16)


def ffn_kernel(
    att, x_ref, accept, w_out, up_a, up_b, down_a, down_b, g1, b1, g2, b2, out, wide, hidden, acc
):
    step = pl.program_id(0)
    shards, rows, width = x_ref.shape
    full = shards * width

    @pl.when(step == 0)
    def _():
        for i in range(shards):
            wide[:, i * width : (i + 1) * width] = att[i]
        total = jnp.dot(wide[...], w_out[...], preferred_element_type=F32)
        for i in range(shards):
            wide[:, i * width : (i + 1) * width] = x_ref[i]
        total = total + wide[...].astype(F32)
        hidden[...] = normalize(total, g1[...], b1[...], full)
        acc[...] = hidden[...].astype(F32)

    h = hidden[...]
    for up, down in ((up_a, down_a), (up_b, down_b)):
        raised = jnp.dot(h, up[0], preferred_element_type=F32)
        active = (0.5 * raised * (1.0 + lax.erf(raised * (0.5**0.5)))).astype(BF16)
        acc[...] += jnp.dot(active, down[0], preferred_element_type=F32)

    @pl.when(step == pl.num_programs(0) - 1)
    def _():
        result = normalize(acc[...], g2[...], b2[...], full)
        chosen = accept[...] != 0
        for i in range(shards):
            out[i] = jnp.where(chosen, result[:, i * width : (i + 1) * width], x_ref[i])


def feed_forward(att, x_parts, accept, w_out, up, down, g1, b1, g2, b2):
    shards, rows, width = x_parts.shape
    full = shards * width

    def fixed(shape):
        return pl.BlockSpec(shape, lambda i: (0,) * len(shape), pipeline_mode=pl.Buffered(1))

    def part(array):
        return pl.BlockSpec((1,) + array.shape[1:], lambda i: (i, 0, 0))

    return pl.pallas_call(
        ffn_kernel,
        grid=(up[0].shape[0],),
        out_shape=jax.ShapeDtypeStruct(x_parts.shape, BF16),
        in_specs=[
            fixed(x_parts.shape),
            fixed(x_parts.shape),
            fixed((rows, 1)),
            fixed(w_out.shape),
            part(up[0]),
            part(up[1]),
            part(down[0]),
            part(down[1]),
        ]
        + [fixed((1, full))] * 4,
        out_specs=pl.BlockSpec(x_parts.shape, lambda i: (0, 0, 0)),
        scratch_shapes=[
            pltpu.VMEM((rows, full), BF16),
            pltpu.VMEM((rows, full), BF16),
            pltpu.VMEM((rows, full), F32),
        ],
        compiler_params=pltpu.CompilerParams(
            dimension_semantics=("arbitrary",), vmem_limit_bytes=48 << 20
        ),
        name="feed_forward",
    )(att, x_parts, accept, w_out, up[0], up[1], down[0], down[1], g1, b1, g2, b2)


def to_all(copies):
    return lax.all_to_all(copies, "mlp", 0, 0, tiled=True)


def core_pair():
    return [(i, i ^ 1) for i in range(lax.axis_size("pages"))]


def per_device(
    embeddings,
    w_query,
    w_key,
    w_value,
    w_global_query,
    w_out,
    w_up,
    w_down,
    norm1_gain,
    norm1_bias,
    norm2_gain,
    norm2_bias,
    cache_keys,
    cache_values,
    lengths,
    page_table,
    accept,
):
    shards = lax.axis_size("mlp")
    me = lax.axis_index("pages")
    shard = lax.axis_index("mlp")
    rows, width = embeddings.shape
    pages, found = pages_to_owners(page_table, cache_keys, cache_values)
    length = lax.dynamic_slice_in_dim(lengths, me, 1, 0)

    core = me % 2
    half = w_up.shape[1] // 2
    up_half = lax.dynamic_slice_in_dim(w_up, core * half, half, 1)
    down_half = lax.dynamic_slice_in_dim(w_down, core * half, half, 0)
    w_out_all = lax.all_gather(w_out, "mlp", axis=0, tiled=True)
    up_mine = lax.all_gather(up_half, "mlp", axis=0)
    down_mine = lax.all_gather(down_half, "mlp", axis=0)
    up_other = lax.ppermute(up_mine, "pages", core_pair())
    down_other = lax.ppermute(down_mine, "pages", core_pair())
    norms = [v.reshape(1, -1) for v in (norm1_gain, norm1_bias, norm2_gain, norm2_bias)]

    x_parts = lax.all_gather(embeddings, "mlp", axis=0)
    for pass_index in range(2):
        attention = attend(
            found, length, x_parts, w_query, w_key, w_value, w_global_query, pages
        )
        x_parts = feed_forward(
            to_all(attention),
            x_parts,
            accept[pass_index].reshape(rows, 1),
            w_out_all,
            (up_mine, up_other),
            (down_mine, down_other),
            *norms,
        )
    return lax.dynamic_index_in_dim(x_parts, shard, 0, keepdims=False)


def solution(mesh):
    return jax.shard_map(
        per_device,
        mesh=mesh,
        in_specs=(
            P("pages", "mlp"),
            P(None, "mlp"),
            P(None, "mlp"),
            P(None, "mlp"),
            P(None, "mlp"),
            P("mlp", None),
            P(None, "mlp"),
            P("mlp", None),
            P(),
            P(),
            P(),
            P(),
            P("pages", None, "mlp"),
            P("pages", None, "mlp"),
            P(),
            P(),
            P(None, "pages"),
        ),
        out_specs=P("pages", "mlp"),
        check_vma=False,
    )
```

```python
import functools

import jax
import jax.numpy as jnp
from jax import lax
from jax.experimental import pallas as pl
from jax.experimental.pallas import tpu as pltpu
from jax.sharding import PartitionSpec as P

HD = 64
BLK = 256
PAGE = 128
EPS = 1e-05
NEG = -1e30
CAP = 2
KEY_BLOCK = 4096
GROUP = 8
PER = 2
LOG2E = 1.4426950408889634
F32 = jnp.float32
BF16 = jnp.bfloat16
VMEM = pl.BlockSpec(memory_space=pltpu.VMEM)
ANY = pl.BlockSpec(memory_space=pl.ANY)
SMEM = pl.BlockSpec(memory_space=pltpu.SMEM)


def routing(page_table, me, holders, slots, hold):
    requests, pages = page_table.shape
    i32 = jnp.int32
    holder_of = jnp.where(page_table >= 0, page_table // slots, -1)
    ids = jnp.arange(holders, dtype=i32)
    page_ids = jnp.arange(pages, dtype=i32)
    on = holder_of[:, None, :] == ids[None, :, None]
    first = jnp.min(jnp.where(on, page_ids[None, None, :], pages), axis=2)
    count = jnp.sum(on.astype(i32), axis=2)
    rank = jnp.sum((first[:, None, :] < first[:, :, None]).astype(i32), axis=2)
    groups = holders // hold
    request_ids = jnp.arange(requests, dtype=i32)
    earlier = request_ids[None, :] < request_ids[:, None]

    def before(sent):
        return jnp.sum((earlier[:, :, None] & sent[None, :, :]).astype(i32), axis=1)

    my_rank = lax.dynamic_slice_in_dim(rank, me, 1, 1)
    my_count = lax.dynamic_slice_in_dim(count, me, 1, 1)
    to = (my_rank % groups == ids[None, :] // hold) & (my_count > ids[None, :] % hold)
    to_turn = before(to)
    mine = holder_of == me
    nth = jnp.sum(
        ((page_ids[None, :, None] > page_ids[None, None, :]) & mine[:, None, :]).astype(i32), axis=2
    )
    local = page_table % slots
    hit = mine[:, None, :] & (nth[:, None, :] == (ids % hold)[None, :, None])
    source = jnp.sum(jnp.where(hit, local[:, None, :], 0), axis=2)

    def send_table(turn):
        want = turn * CAP + jnp.arange(CAP, dtype=i32)
        chosen = to[:, :, None] & (to_turn[:, :, None] == want[None, None, :])
        return jnp.sum(jnp.where(chosen, source[:, :, None], 0), axis=0).reshape(-1)

    places = pages // holders
    came = (rank % groups == me // hold) & (count > me % hold)
    came_turn = before(came)

    def pass_table(turn):
        place = rank // groups
        chosen = (
            came[:, :, None]
            & (place[:, :, None] == jnp.arange(places, dtype=i32)[None, None, :])
            & (came_turn // CAP == turn)[:, :, None]
        )
        origin = ids[None, :] * CAP + came_turn % CAP + 1
        return (jnp.sum(jnp.where(chosen, origin[:, :, None], 0), axis=1) - 1).reshape(-1)

    all_to = (rank[:, :, None] % groups == ids[None, None, :] // hold) & (
        count[:, :, None] > ids[None, None, :] % hold
    )
    rounds = (jnp.max(jnp.sum(all_to.astype(i32), axis=0)) + CAP - 1) // CAP

    own_holder = lax.dynamic_slice_in_dim(holder_of, me, 1, 0)[0]
    own_rank = lax.dynamic_slice_in_dim(rank, me, 1, 0)[0]
    page_rank = jnp.sum(
        jnp.where(own_holder[:, None] == ids[None, :], own_rank[None, :], 0), axis=1
    )
    page_nth = jnp.sum(
        (
            (page_ids[None, :] < page_ids[:, None])
            & (own_holder[None, :] == own_holder[:, None])
        ).astype(i32),
        axis=1,
    )
    unit = page_rank * hold + page_nth
    found = jnp.where(own_holder >= 0, (unit % holders) * places + unit // holders, 0)
    return send_table, pass_table, rounds, found


def staged(total, group, load, stage, packed, got_sem, put_sem):
    for g in range(total // group):
        for i in range(g * group, (g + 1) * group):
            load(i, got_sem.at[g])
    for g in range(total // group):
        part = pl.ds(g * group, group)
        pltpu.make_async_copy(stage.at[part], stage.at[part], got_sem.at[g]).wait()
        pltpu.make_async_copy(stage.at[part], packed.at[part], put_sem).start()
    pltpu.make_async_copy(stage, packed, put_sem).wait()


def pack_kernel(table, keys, values, packed, stage, got_sem, put_sem):
    def load(i, sem):
        slot = table[i]
        pltpu.make_async_copy(keys.at[slot], stage.at[i, 0], sem).start()
        pltpu.make_async_copy(values.at[slot], stage.at[i, 1], sem).start()

    staged(stage.shape[0], GROUP, load, stage, packed, got_sem, put_sem)


def repack_kernel(table, got, packed, stage, got_sem, put_sem):
    def load(i, sem):
        pltpu.make_async_copy(got.at[jnp.maximum(table[i], 0)], stage.at[i], sem).start()

    staged(stage.shape[0], GROUP, load, stage, packed, got_sem, put_sem)


def staged_call(kernel, name, table, page_shape, *arrays):
    shape = (table.shape[0], 2) + page_shape
    return pl.pallas_call(
        kernel,
        out_shape=jax.ShapeDtypeStruct(shape, BF16),
        in_specs=[SMEM] + [ANY] * len(arrays),
        out_specs=ANY,
        scratch_shapes=[
            pltpu.VMEM(shape, BF16),
            pltpu.SemaphoreType.DMA((shape[0] // GROUP,)),
            pltpu.SemaphoreType.DMA,
        ],
        compiler_params=pltpu.CompilerParams(vmem_limit_bytes=60 << 20),
        name=name,
    )(table, *arrays)


def pack_pages(table, keys, values):
    return staged_call(pack_kernel, "pack_pages", table, keys.shape[1:], keys, values)


def repack_pages(table, got):
    return staged_call(repack_kernel, "repack_pages", table, got.shape[2:], got)


def exchange(pages):
    holders = lax.axis_size("pages")
    shape = pages.shape
    sent = lax.all_to_all(
        pages.reshape((holders, shape[0] // holders) + shape[1:]), "pages", 0, 0, tiled=True
    )
    return sent.reshape(shape)


def pages_to_owners(page_table, keys, values, own):
    holders = lax.axis_size("pages")
    me = lax.axis_index("pages")
    hold = 8
    send_table, pass_table, rounds, found = routing(page_table, me, holders, keys.shape[0], hold)
    packed, own = lax.optimization_barrier((pack_pages(send_table(0), keys, values), own))
    x_parts = lax.all_gather(own, "mlp", axis=0)
    first, x_parts = lax.optimization_barrier((exchange(packed), x_parts))
    middle = repack_pages(pass_table(0), first)

    def further(turn, middle):
        got = exchange(pack_pages(send_table(turn), keys, values))
        table = pass_table(turn)
        return jnp.where((table >= 0)[:, None, None, None], repack_pages(table, got), middle)

    middle = lax.fori_loop(1, rounds, further, middle)
    return exchange(middle), found, x_parts


def two_heads(rows):
    lane = lax.broadcasted_iota(jnp.int32, rows.shape, 1)
    low = jnp.where(lane < HD, rows, 0.0)
    high = jnp.where(lane < HD, 0.0, rows)
    return jnp.concatenate([low, high], axis=0).astype(BF16)


def attention_kernel(
    found, length, x_ref, wq, wk, wv, wg, pages, out, x_all, key_buf, value_buf, kept, peak, acc, ksem, vsem
):
    per_block = KEY_BLOCK // PAGE
    shards = x_ref.shape[0]
    width = x_ref.shape[2]
    limit = length[0]
    blocks = (limit + KEY_BLOCK - 1) // KEY_BLOCK

    def block_rows(block):
        return pl.ds(pl.multiple_of(block * KEY_BLOCK, KEY_BLOCK), KEY_BLOCK)

    def fetch(block, carry, part, buf, sem):
        for i in range(per_block):
            page = block * per_block + i
            rows = pl.ds(pl.multiple_of(page * PAGE, PAGE), PAGE)
            pltpu.make_async_copy(pages.at[found[page], part], buf.at[rows], sem.at[block]).start()
        return carry

    lax.fori_loop(0, blocks, functools.partial(fetch, part=0, buf=key_buf, sem=ksem), 0)
    lax.fori_loop(0, blocks, functools.partial(fetch, part=1, buf=value_buf, sem=vsem), 0)
    for i in range(shards):
        x_all[:, i * width : (i + 1) * width] = x_ref[i]
    x = x_all[...]

    def project(matrix):
        return jnp.dot(x, matrix[...], preferred_element_type=F32).astype(BF16)

    scale = HD ** (-0.5)
    queries = two_heads(project(wq).astype(F32) * scale)
    global_rows = two_heads(project(wg).astype(F32) * scale)
    key_rows = project(wk)
    value_rows = project(wv)

    def scores_of(left, keys):
        return lax.dot_general(
            left, keys, (((1,), (1,)), ((), ())), preferred_element_type=F32
        ) * LOG2E

    def fold(scores):
        parts = [scores[:, i : i + 128] for i in range(0, scores.shape[1], 128)]
        while len(parts) > 1:
            parts = [jnp.maximum(*parts[i : i + 2]) for i in range(0, len(parts), 2)]
        return parts[0]

    def weigh(scores, top, values):
        ones = jnp.ones(values.shape, BF16)
        weights = jnp.exp2(scores - top).astype(BF16)
        return jnp.dot(
            weights, jnp.concatenate([values, ones], axis=1), preferred_element_type=F32
        )

    own = scores_of(queries, key_rows)
    peak[...] = fold(own)

    def score_step(block, carry):
        rows = block_rows(block)
        pltpu.make_async_copy(key_buf.at[rows], key_buf.at[rows], ksem.at[block]).wait()
        scores = scores_of(global_rows, key_buf[rows, :])
        position = block * KEY_BLOCK + lax.broadcasted_iota(jnp.int32, scores.shape, 1)
        scores = jnp.where(position < limit, scores, NEG)
        kept[block] = scores
        peak[...] = jnp.maximum(peak[...], fold(scores))
        return carry

    lax.fori_loop(0, blocks, score_step, 0)
    top = jnp.max(peak[...], axis=1, keepdims=True)
    peak[...] = jnp.broadcast_to(top, peak.shape)
    acc[...] = weigh(own, top, value_rows)

    def weigh_step(block, carry):
        rows = block_rows(block)
        pltpu.make_async_copy(value_buf.at[rows], value_buf.at[rows], vsem.at[block]).wait()
        acc[...] += weigh(kept[block], peak[:, :1], value_buf[rows, :])
        return carry

    lax.fori_loop(0, blocks, weigh_step, 0)
    rows = x_ref.shape[1]
    total = acc[...]
    ratio = total[:, :width] / total[:, width:]
    lane = lax.broadcasted_iota(jnp.int32, (rows, width), 1)
    result = jnp.where(lane < HD, ratio[:rows], ratio[rows:]).astype(BF16)
    for i in range(shards):
        out[i] = result


def attend(found, length, x_parts, wq, wk, wv, wg, pages):
    shards, rows, width = x_parts.shape
    longest = found.shape[0] * PAGE
    return pl.pallas_call(
        attention_kernel,
        out_shape=jax.ShapeDtypeStruct(x_parts.shape, BF16),
        in_specs=[SMEM, SMEM, VMEM, VMEM, VMEM, VMEM, VMEM, ANY],
        out_specs=VMEM,
        scratch_shapes=[
            pltpu.VMEM((rows, shards * width), BF16),
            pltpu.VMEM((longest, width), BF16),
            pltpu.VMEM((longest, width), BF16),
            pltpu.VMEM((longest // KEY_BLOCK, 2 * rows, KEY_BLOCK), F32),
            pltpu.VMEM((2 * rows, 128), F32),
            pltpu.VMEM((2 * rows, 2 * width), F32),
            pltpu.SemaphoreType.DMA((longest // KEY_BLOCK,)),
            pltpu.SemaphoreType.DMA((longest // KEY_BLOCK,)),
        ],
        compiler_params=pltpu.CompilerParams(vmem_limit_bytes=56 << 20),
        name="attention",
    )(found, length, x_parts, wq, wk, wv, wg, pages)


def normalize(total, gain, bias, width):
    mean = jnp.sum(total, axis=1, keepdims=True) * (1.0 / width)
    square = jnp.sum(total * total, axis=1, keepdims=True) * (1.0 / width)
    inverse = lax.rsqrt(square - mean * mean + EPS)
    return ((total - mean) * inverse * gain + bias).astype(BF16)


def ffn_kernel(
    att, x_ref, accept, w_out, up_a, up_b, down_a, down_b, g1, b1, g2, b2, out, wide, hidden, acc
):
    step = pl.program_id(0)
    shards, rows, width = x_ref.shape
    full = shards * width

    @pl.when(step == 0)
    def _():
        for i in range(shards):
            wide[:, i * width : (i + 1) * width] = att[i]
        total = jnp.dot(wide[...], w_out[...], preferred_element_type=F32)
        for i in range(shards):
            wide[:, i * width : (i + 1) * width] = x_ref[i]
        total = total + wide[...].astype(F32)
        hidden[...] = normalize(total, g1[...], b1[...], full)
        acc[...] = hidden[...].astype(F32)

    h = hidden[...]
    raised = [
        jnp.dot(h, up[i], preferred_element_type=F32)
        for i in range(up_a.shape[0])
        for up in (up_a, up_b)
    ]
    active = [(0.5 * v * (1.0 + lax.erf(v * (0.5**0.5)))).astype(BF16) for v in raised]
    downs = [down[i] for i in range(up_a.shape[0]) for down in (down_a, down_b)]
    acc[...] += jnp.dot(
        jnp.concatenate(active, axis=1),
        jnp.concatenate(downs, axis=0),
        preferred_element_type=F32,
    )

    @pl.when(step == pl.num_programs(0) - 1)
    def _():
        result = normalize(acc[...], g2[...], b2[...], full)
        chosen = accept[...] != 0
        for i in range(shards):
            out[i] = jnp.where(chosen, result[:, i * width : (i + 1) * width], x_ref[i])


def feed_forward(att, x_parts, accept, w_out, up, down, g1, b1, g2, b2):
    shards, rows, width = x_parts.shape
    full = shards * width

    def fixed(shape):
        return pl.BlockSpec(shape, lambda i: (0,) * len(shape), pipeline_mode=pl.Buffered(1))

    def part(array):
        return pl.BlockSpec((PER,) + array.shape[1:], lambda i: (i, 0, 0))

    return pl.pallas_call(
        ffn_kernel,
        grid=(up[0].shape[0] // PER,),
        out_shape=jax.ShapeDtypeStruct(x_parts.shape, BF16),
        in_specs=[
            fixed(x_parts.shape),
            fixed(x_parts.shape),
            fixed((rows, 1)),
            fixed(w_out.shape),
            part(up[0]),
            part(up[1]),
            part(down[0]),
            part(down[1]),
        ]
        + [fixed((1, full))] * 4,
        out_specs=pl.BlockSpec(x_parts.shape, lambda i: (0, 0, 0)),
        scratch_shapes=[
            pltpu.VMEM((rows, full), BF16),
            pltpu.VMEM((rows, full), BF16),
            pltpu.VMEM((rows, full), F32),
        ],
        compiler_params=pltpu.CompilerParams(
            dimension_semantics=("arbitrary",), vmem_limit_bytes=60 << 20
        ),
        name="feed_forward",
    )(att, x_parts, accept, w_out, up[0], up[1], down[0], down[1], g1, b1, g2, b2)


def to_all(copies):
    return lax.all_to_all(copies, "mlp", 0, 0, tiled=True)


def core_pair():
    return [(i, i ^ 1) for i in range(lax.axis_size("pages"))]


def per_device(
    embeddings,
    w_query,
    w_key,
    w_value,
    w_global_query,
    w_out,
    w_up,
    w_down,
    norm1_gain,
    norm1_bias,
    norm2_gain,
    norm2_bias,
    cache_keys,
    cache_values,
    lengths,
    page_table,
    accept,
):
    shards = lax.axis_size("mlp")
    me = lax.axis_index("pages")
    shard = lax.axis_index("mlp")
    rows, width = embeddings.shape
    pages, found, x_parts = pages_to_owners(page_table, cache_keys, cache_values, embeddings)
    length = lax.dynamic_slice_in_dim(lengths, me, 1, 0)

    core = me % 2
    half = w_up.shape[1] // 2
    up_half = lax.dynamic_slice_in_dim(w_up, core * half, half, 1)
    down_half = lax.dynamic_slice_in_dim(w_down, core * half, half, 0)
    w_out_all = lax.all_gather(w_out, "mlp", axis=0, tiled=True)
    up_mine = lax.all_gather(up_half, "mlp", axis=0)
    down_mine = lax.all_gather(down_half, "mlp", axis=0)
    up_other = lax.ppermute(up_mine, "pages", core_pair())
    down_other = lax.ppermute(down_mine, "pages", core_pair())
    norms = [v.reshape(1, -1) for v in (norm1_gain, norm1_bias, norm2_gain, norm2_bias)]

    for pass_index in range(2):
        attention = attend(
            found, length, x_parts, w_query, w_key, w_value, w_global_query, pages
        )
        x_parts = feed_forward(
            to_all(attention),
            x_parts,
            accept[pass_index].reshape(rows, 1),
            w_out_all,
            (up_mine, up_other),
            (down_mine, down_other),
            *norms,
        )
    return lax.dynamic_index_in_dim(x_parts, shard, 0, keepdims=False)


def solution(mesh):
    return jax.shard_map(
        per_device,
        mesh=mesh,
        in_specs=(
            P("pages", "mlp"),
            P(None, "mlp"),
            P(None, "mlp"),
            P(None, "mlp"),
            P(None, "mlp"),
            P("mlp", None),
            P(None, "mlp"),
            P("mlp", None),
            P(),
            P(),
            P(),
            P(),
            P("pages", None, "mlp"),
            P("pages", None, "mlp"),
            P(),
            P(),
            P(None, "pages"),
        ),
        out_specs=P("pages", "mlp"),
        check_vma=False,
    )
```

```python
import functools

import jax
import jax.numpy as jnp
from jax import lax
from jax.experimental import pallas as pl
from jax.experimental.pallas import tpu as pltpu
from jax.sharding import PartitionSpec as P

HD = 64
BLK = 256
PAGE = 128
EPS = 1e-05
NEG = -1e30
CAP = 2
KEY_BLOCK = 4096
GROUP = 8
HOLD = 8
PER = 2
LOG2E = 1.4426950408889634
F32 = jnp.float32
BF16 = jnp.bfloat16
VMEM = pl.BlockSpec(memory_space=pltpu.VMEM)
ANY = pl.BlockSpec(memory_space=pl.ANY)
SMEM = pl.BlockSpec(memory_space=pltpu.SMEM)


def routing(page_table, me, holders, slots, hold):
    requests, pages = page_table.shape
    i32 = jnp.int32
    holder_of = jnp.where(page_table >= 0, page_table // slots, -1)
    ids = jnp.arange(holders, dtype=i32)
    page_ids = jnp.arange(pages, dtype=i32)
    on = holder_of[:, None, :] == ids[None, :, None]
    first = jnp.min(jnp.where(on, page_ids[None, None, :], pages), axis=2)
    count = jnp.sum(on.astype(i32), axis=2)
    rank = jnp.sum((first[:, None, :] < first[:, :, None]).astype(i32), axis=2)
    groups = holders // hold
    request_ids = jnp.arange(requests, dtype=i32)
    earlier = request_ids[None, :] < request_ids[:, None]

    def before(sent):
        return jnp.sum((earlier[:, :, None] & sent[None, :, :]).astype(i32), axis=1)

    places = pages // holders
    came = (rank % groups == me // hold) & (count > me % hold)
    came_turn = before(came)

    def pass_table(turn):
        place = rank // groups
        chosen = (
            came[:, :, None]
            & (place[:, :, None] == jnp.arange(places, dtype=i32)[None, None, :])
            & (came_turn // CAP == turn)[:, :, None]
        )
        origin = ids[None, :] * CAP + came_turn % CAP + 1
        return (jnp.sum(jnp.where(chosen, origin[:, :, None], 0), axis=1) - 1).reshape(-1)

    all_to = (rank[:, :, None] % groups == ids[None, None, :] // hold) & (
        count[:, :, None] > ids[None, None, :] % hold
    )
    rounds = (jnp.max(jnp.sum(all_to.astype(i32), axis=0)) + CAP - 1) // CAP

    own_holder = lax.dynamic_slice_in_dim(holder_of, me, 1, 0)[0]
    own_rank = lax.dynamic_slice_in_dim(rank, me, 1, 0)[0]
    page_rank = jnp.sum(
        jnp.where(own_holder[:, None] == ids[None, :], own_rank[None, :], 0), axis=1
    )
    page_nth = jnp.sum(
        (
            (page_ids[None, :] < page_ids[:, None])
            & (own_holder[None, :] == own_holder[:, None])
        ).astype(i32),
        axis=1,
    )
    unit = page_rank * hold + page_nth
    found = jnp.where(own_holder >= 0, (unit % holders) * places + unit // holders, 0)
    return pass_table, rounds, found


def staged(total, group, load, stage, packed, got_sem, put_sem):
    for g in range(total // group):
        for i in range(g * group, (g + 1) * group):
            load(i, got_sem.at[g])
    for g in range(total // group):
        part = pl.ds(g * group, group)
        pltpu.make_async_copy(stage.at[part], stage.at[part], got_sem.at[g]).wait()
        pltpu.make_async_copy(stage.at[part], packed.at[part], put_sem).start()
    pltpu.make_async_copy(stage, packed, put_sem).wait()


def pack_kernel(
    where_and_turn, page_table, keys, values, packed, table_v, table, stage, table_sem, got_sem, put_sem
):
    me, turn = where_and_turn[0], where_and_turn[1]
    requests, pages = page_table.shape
    slots = keys.shape[0]
    holders = packed.shape[0] // CAP
    groups = holders // HOLD
    i32 = jnp.int32
    slot_of = page_table[...]
    holder_of = jnp.where(slot_of >= 0, slot_of // slots, -1)
    local = slot_of % slots
    page_ids = lax.broadcasted_iota(i32, slot_of.shape, 1)
    mine = holder_of == me

    def first_of(on):
        return jnp.min(jnp.where(on, page_ids, pages), axis=1, keepdims=True)

    own_first = first_of(mine)
    rank = jnp.zeros((requests, 1), i32)
    for holder in range(holders):
        rank += (first_of(holder_of == holder) < own_first).astype(i32)
    mine_f = mine.astype(F32)
    count = jnp.sum(mine_f, axis=1, keepdims=True).astype(i32)
    before = lax.broadcasted_iota(i32, (pages, pages), 0) < lax.broadcasted_iota(
        i32, (pages, pages), 1
    )
    nth = jnp.dot(mine_f, before.astype(F32), preferred_element_type=F32).astype(i32)
    target = lax.broadcasted_iota(i32, (requests, holders), 1)
    to = (rank % groups == target // HOLD) & (count > target % HOLD)
    source = jnp.zeros((requests, holders), i32)
    for k in range(HOLD):
        hit = jnp.sum(jnp.where(mine & (nth == k), local, 0), axis=1, keepdims=True)
        source = jnp.where(target % HOLD == k, hit, source)
    earlier = lax.broadcasted_iota(i32, (requests, requests), 1) < lax.broadcasted_iota(
        i32, (requests, requests), 0
    )
    order = jnp.dot(
        earlier.astype(F32), to.astype(F32), preferred_element_type=F32
    ).astype(i32)
    for place in range(CAP):
        chosen = to & (order == turn * CAP + place)
        table_v[place : place + 1, 0:holders] = jnp.sum(
            jnp.where(chosen, source, 0), axis=0, keepdims=True
        )
    copy = pltpu.make_async_copy(table_v, table, table_sem)
    copy.start()
    copy.wait()

    def load(i, sem):
        slot = table[i % CAP, i // CAP]
        pltpu.make_async_copy(keys.at[slot], stage.at[i, 0], sem).start()
        pltpu.make_async_copy(values.at[slot], stage.at[i, 1], sem).start()

    staged(stage.shape[0], GROUP, load, stage, packed, got_sem, put_sem)


def repack_kernel(table, got, packed, stage, got_sem, put_sem):
    def load(i, sem):
        pltpu.make_async_copy(got.at[jnp.maximum(table[i], 0)], stage.at[i], sem).start()

    staged(stage.shape[0], GROUP, load, stage, packed, got_sem, put_sem)


def staging(shape):
    return [
        pltpu.VMEM(shape, BF16),
        pltpu.SemaphoreType.DMA((shape[0] // GROUP,)),
        pltpu.SemaphoreType.DMA,
    ]


def pack_pages(me, turn, page_table, keys, values):
    shape = (lax.axis_size("pages") * CAP, 2) + keys.shape[1:]
    return pl.pallas_call(
        pack_kernel,
        out_shape=jax.ShapeDtypeStruct(shape, BF16),
        in_specs=[SMEM, VMEM, ANY, ANY],
        out_specs=ANY,
        scratch_shapes=[
            pltpu.VMEM((8, 128), jnp.int32),
            pltpu.SMEM((8, 128), jnp.int32),
            staging(shape)[0],
            pltpu.SemaphoreType.DMA,
        ]
        + staging(shape)[1:],
        compiler_params=pltpu.CompilerParams(vmem_limit_bytes=60 << 20),
        name="pack_pages",
    )(jnp.stack([me, turn]).astype(jnp.int32), page_table, keys, values)


def repack_pages(table, got):
    return pl.pallas_call(
        repack_kernel,
        out_shape=jax.ShapeDtypeStruct(got.shape, BF16),
        in_specs=[SMEM, ANY],
        out_specs=ANY,
        scratch_shapes=staging(got.shape),
        compiler_params=pltpu.CompilerParams(vmem_limit_bytes=60 << 20),
        name="repack_pages",
    )(table, got)


def exchange(pages):
    holders = lax.axis_size("pages")
    shape = pages.shape
    sent = lax.all_to_all(
        pages.reshape((holders, shape[0] // holders) + shape[1:]), "pages", 0, 0, tiled=True
    )
    return sent.reshape(shape)


def pages_to_owners(page_table, keys, values, later):
    holders = lax.axis_size("pages")
    me = lax.axis_index("pages")
    packed, table, later = lax.optimization_barrier(
        (pack_pages(me, 0, page_table, keys, values), page_table, later)
    )
    pass_table, rounds, found = routing(table, me, holders, keys.shape[0], HOLD)
    x_parts = lax.all_gather(later[0], "mlp", axis=0)
    first, x_parts = lax.optimization_barrier((exchange(packed), x_parts))
    middle = repack_pages(pass_table(0), first)

    def further(turn, middle):
        got = exchange(pack_pages(me, turn, page_table, keys, values))
        table = pass_table(turn)
        return jnp.where((table >= 0)[:, None, None, None], repack_pages(table, got), middle)

    middle = lax.fori_loop(1, rounds, further, middle)
    return exchange(middle), found, x_parts, later[1:]


def two_heads(rows):
    lane = lax.broadcasted_iota(jnp.int32, rows.shape, 1)
    low = jnp.where(lane < HD, rows, 0.0)
    high = jnp.where(lane < HD, 0.0, rows)
    return jnp.concatenate([low, high], axis=0).astype(BF16)


def project_kernel(x_ref, wq, wk, wv, wg, queries, global_rows, key_rows, value_rows, x_all):
    shards, _, width = x_ref.shape
    for i in range(shards):
        x_all[:, i * width : (i + 1) * width] = x_ref[i]
    x = x_all[...]

    def project(matrix):
        return jnp.dot(x, matrix[...], preferred_element_type=F32).astype(BF16)

    scale = HD ** (-0.5)
    queries[...] = two_heads(project(wq).astype(F32) * scale)
    global_rows[...] = two_heads(project(wg).astype(F32) * scale)
    key_rows[...] = project(wk)
    value_rows[...] = project(wv)


def project_all(x_parts, wq, wk, wv, wg):
    shards, rows, width = x_parts.shape
    doubled = jax.ShapeDtypeStruct((2 * rows, width), BF16)
    single = jax.ShapeDtypeStruct((rows, width), BF16)
    return pl.pallas_call(
        project_kernel,
        out_shape=(doubled, doubled, single, single),
        in_specs=[VMEM] * 5,
        out_specs=(VMEM,) * 4,
        scratch_shapes=[pltpu.VMEM((rows, shards * width), BF16)],
        name="project",
    )(x_parts, wq, wk, wv, wg)


def attention_kernel(
    found,
    length,
    queries,
    global_rows,
    key_rows,
    value_rows,
    pages,
    out,
    key_buf,
    value_buf,
    kept,
    peak,
    acc,
    ksem,
    vsem,
):
    per_block = KEY_BLOCK // PAGE
    shards, rows, width = out.shape
    limit = length[0]
    blocks = (limit + KEY_BLOCK - 1) // KEY_BLOCK

    def block_rows(block):
        return pl.ds(pl.multiple_of(block * KEY_BLOCK, KEY_BLOCK), KEY_BLOCK)

    def fetch(block, carry, part, buf, sem):
        for i in range(per_block):
            page = block * per_block + i
            rows = pl.ds(pl.multiple_of(page * PAGE, PAGE), PAGE)
            pltpu.make_async_copy(pages.at[found[page], part], buf.at[rows], sem.at[block]).start()
        return carry

    lax.fori_loop(0, blocks, functools.partial(fetch, part=0, buf=key_buf, sem=ksem), 0)
    lax.fori_loop(0, blocks, functools.partial(fetch, part=1, buf=value_buf, sem=vsem), 0)
    def scores_of(left, keys):
        return lax.dot_general(
            left, keys, (((1,), (1,)), ((), ())), preferred_element_type=F32
        ) * LOG2E

    def fold(scores):
        parts = [scores[:, i : i + 128] for i in range(0, scores.shape[1], 128)]
        while len(parts) > 1:
            parts = [jnp.maximum(*parts[i : i + 2]) for i in range(0, len(parts), 2)]
        return parts[0]

    def weigh(scores, top, values):
        ones = jnp.ones(values.shape, BF16)
        weights = jnp.exp2(scores - top).astype(BF16)
        return jnp.dot(
            weights, jnp.concatenate([values, ones], axis=1), preferred_element_type=F32
        )

    own = scores_of(queries[...], key_rows[...])
    peak[...] = fold(own)

    def score_step(block, carry):
        part = key_buf.at[block_rows(block)]
        pltpu.make_async_copy(part, part, ksem.at[block]).wait()
        scores = scores_of(global_rows[...], key_buf[block_rows(block), :])
        position = block * KEY_BLOCK + lax.broadcasted_iota(jnp.int32, scores.shape, 1)
        scores = jnp.where(position < limit, scores, NEG)
        kept[block] = scores
        peak[...] = jnp.maximum(peak[...], fold(scores))
        return carry

    lax.fori_loop(0, blocks, score_step, 0)
    top = jnp.max(peak[...], axis=1, keepdims=True)
    peak[...] = jnp.broadcast_to(top, peak.shape)
    acc[...] = weigh(own, top, value_rows[...])

    def weigh_step(block, carry):
        part = value_buf.at[block_rows(block)]
        pltpu.make_async_copy(part, part, vsem.at[block]).wait()
        acc[...] += weigh(kept[block], peak[:, :1], value_buf[block_rows(block), :])
        return carry

    lax.fori_loop(0, blocks, weigh_step, 0)
    total = acc[...]
    ratio = total[:, :width] / total[:, width:]
    lane = lax.broadcasted_iota(jnp.int32, (rows, width), 1)
    result = jnp.where(lane < HD, ratio[:rows], ratio[rows:]).astype(BF16)
    for i in range(shards):
        out[i] = result


def attend(found, length, shards, queries, global_rows, key_rows, value_rows, pages):
    rows, width = key_rows.shape
    longest = found.shape[0] * PAGE
    return pl.pallas_call(
        attention_kernel,
        out_shape=jax.ShapeDtypeStruct((shards, rows, width), BF16),
        in_specs=[SMEM, SMEM] + [VMEM] * 4 + [ANY],
        out_specs=VMEM,
        scratch_shapes=[
            pltpu.VMEM((longest, width), BF16),
            pltpu.VMEM((longest, width), BF16),
            pltpu.VMEM((longest // KEY_BLOCK, 2 * rows, KEY_BLOCK), F32),
            pltpu.VMEM((2 * rows, 128), F32),
            pltpu.VMEM((2 * rows, 2 * width), F32),
            pltpu.SemaphoreType.DMA((longest // KEY_BLOCK,)),
            pltpu.SemaphoreType.DMA((longest // KEY_BLOCK,)),
        ],
        compiler_params=pltpu.CompilerParams(vmem_limit_bytes=56 << 20),
        name="attention",
    )(found, length, queries, global_rows, key_rows, value_rows, pages)


def normalize(total, gain, bias, width):
    mean = jnp.sum(total, axis=1, keepdims=True) * (1.0 / width)
    square = jnp.sum(total * total, axis=1, keepdims=True) * (1.0 / width)
    inverse = lax.rsqrt(square - mean * mean + EPS)
    return ((total - mean) * inverse * gain + bias).astype(BF16)


def ffn_kernel(
    column, att, x_ref, accept, w_out, up_a, up_b, down_a, down_b, g1, b1, g2, b2, out, wide, hidden, acc
):
    step = pl.program_id(0)
    shards, rows, width = x_ref.shape
    full = shards * width

    @pl.when(step == 0)
    def _():
        for i in range(shards):
            wide[:, i * width : (i + 1) * width] = att[i]
        total = jnp.dot(wide[...], w_out[...], preferred_element_type=F32)
        for i in range(shards):
            wide[:, i * width : (i + 1) * width] = x_ref[i]
        total = total + wide[...].astype(F32)
        hidden[...] = normalize(total, g1[...], b1[...], full)
        acc[...] = hidden[...].astype(F32)

    h = hidden[...]
    raised = [
        jnp.dot(h, up[i], preferred_element_type=F32)
        for i in range(up_a.shape[0])
        for up in (up_a, up_b)
    ]
    active = [(0.5 * v * (1.0 + lax.erf(v * (0.5**0.5)))).astype(BF16) for v in raised]
    downs = [down[i] for i in range(up_a.shape[0]) for down in (down_a, down_b)]
    acc[...] += jnp.dot(
        jnp.concatenate(active, axis=1),
        jnp.concatenate(downs, axis=0),
        preferred_element_type=F32,
    )

    @pl.when(step == pl.num_programs(0) - 1)
    def _():
        result = normalize(acc[...], g2[...], b2[...], full)
        chosen = accept[...] != 0
        if out.shape[0] == shards:
            for i in range(shards):
                out[i] = jnp.where(chosen, result[:, i * width : (i + 1) * width], x_ref[i])
        else:
            for i in range(shards):

                @pl.when(column[0] == i)
                def _():
                    out[0] = jnp.where(chosen, result[:, i * width : (i + 1) * width], x_ref[i])


def feed_forward(column, outs, att, x_parts, accept, w_out, up, down, g1, b1, g2, b2):
    shards, rows, width = x_parts.shape
    full = shards * width

    def fixed(shape):
        return pl.BlockSpec(shape, lambda i: (0,) * len(shape), pipeline_mode=pl.Buffered(1))

    def part(array):
        return pl.BlockSpec((PER,) + array.shape[1:], lambda i: (i, 0, 0))

    return pl.pallas_call(
        ffn_kernel,
        grid=(up[0].shape[0] // PER,),
        out_shape=jax.ShapeDtypeStruct((outs, rows, width), BF16),
        in_specs=[
            SMEM,
            fixed(x_parts.shape),
            fixed(x_parts.shape),
            fixed((rows, 1)),
            fixed(w_out.shape),
            part(up[0]),
            part(up[1]),
            part(down[0]),
            part(down[1]),
        ]
        + [fixed((1, full))] * 4,
        out_specs=pl.BlockSpec((outs, rows, width), lambda i: (0, 0, 0)),
        scratch_shapes=[
            pltpu.VMEM((rows, full), BF16),
            pltpu.VMEM((rows, full), BF16),
            pltpu.VMEM((rows, full), F32),
        ],
        compiler_params=pltpu.CompilerParams(
            dimension_semantics=("arbitrary",), vmem_limit_bytes=60 << 20
        ),
        name="feed_forward",
    )(column, att, x_parts, accept, w_out, up[0], up[1], down[0], down[1], g1, b1, g2, b2)


def to_all(copies):
    return lax.all_to_all(copies, "mlp", 0, 0, tiled=True)


def core_pair():
    return [(i, i ^ 1) for i in range(lax.axis_size("pages"))]


def per_device(
    embeddings,
    w_query,
    w_key,
    w_value,
    w_global_query,
    w_out,
    w_up,
    w_down,
    norm1_gain,
    norm1_bias,
    norm2_gain,
    norm2_bias,
    cache_keys,
    cache_values,
    lengths,
    page_table,
    accept,
):
    shards = lax.axis_size("mlp")
    me = lax.axis_index("pages")
    shard = lax.axis_index("mlp")
    rows, width = embeddings.shape
    pages, found, x_parts, (w_up, w_down, w_out) = pages_to_owners(
        page_table, cache_keys, cache_values, (embeddings, w_up, w_down, w_out)
    )
    length = lax.dynamic_slice_in_dim(lengths, me, 1, 0)

    core = me % 2
    half = w_up.shape[1] // 2
    up_half = lax.dynamic_slice_in_dim(w_up, core * half, half, 1)
    down_half = lax.dynamic_slice_in_dim(w_down, core * half, half, 0)
    w_out_all = lax.all_gather(w_out, "mlp", axis=0, tiled=True)
    up_mine = lax.all_gather(up_half, "mlp", axis=0)
    down_mine = lax.all_gather(down_half, "mlp", axis=0)
    up_other = lax.ppermute(up_mine, "pages", core_pair())
    down_other = lax.ppermute(down_mine, "pages", core_pair())
    norms = [v.reshape(1, -1) for v in (norm1_gain, norm1_bias, norm2_gain, norm2_bias)]

    column = shard.reshape(1).astype(jnp.int32)
    for pass_index in range(2):
        projected = project_all(x_parts, w_query, w_key, w_value, w_global_query)
        attention = attend(found, length, shards, *projected, pages)
        x_parts = feed_forward(
            column,
            shards if pass_index == 0 else 1,
            to_all(attention),
            x_parts,
            accept[pass_index].reshape(rows, 1),
            w_out_all,
            (up_mine, up_other),
            (down_mine, down_other),
            *norms,
        )
    return x_parts.reshape(rows, width)


def solution(mesh):
    return jax.shard_map(
        per_device,
        mesh=mesh,
        in_specs=(
            P("pages", "mlp"),
            P(None, "mlp"),
            P(None, "mlp"),
            P(None, "mlp"),
            P(None, "mlp"),
            P("mlp", None),
            P(None, "mlp"),
            P("mlp", None),
            P(),
            P(),
            P(),
            P(),
            P("pages", None, "mlp"),
            P("pages", None, "mlp"),
            P(),
            P(),
            P(None, "pages"),
        ),
        out_specs=P("pages", "mlp"),
        check_vma=False,
    )
```

```python
import functools

import jax
import jax.numpy as jnp
from jax import lax
from jax.experimental import pallas as pl
from jax.experimental.pallas import tpu as pltpu
from jax.sharding import PartitionSpec as P

HD = 64
BLK = 256
PAGE = 128
EPS = 1e-05
NEG = -1e30
CAP = 2
KEY_BLOCK = 4096
GROUP = 8
HOLD = 8
PER = 2
LOG2E = 1.4426950408889634
F32 = jnp.float32
BF16 = jnp.bfloat16
VMEM = pl.BlockSpec(memory_space=pltpu.VMEM)
ANY = pl.BlockSpec(memory_space=pl.ANY)
SMEM = pl.BlockSpec(memory_space=pltpu.SMEM)


def routing(page_table, me, holders, slots, hold):
    requests, pages = page_table.shape
    i32 = jnp.int32
    holder_of = jnp.where(page_table >= 0, page_table // slots, -1)
    ids = jnp.arange(holders, dtype=i32)
    page_ids = jnp.arange(pages, dtype=i32)
    on = holder_of[:, None, :] == ids[None, :, None]
    first = jnp.min(jnp.where(on, page_ids[None, None, :], pages), axis=2)
    count = jnp.sum(on.astype(i32), axis=2)
    rank = jnp.sum((first[:, None, :] < first[:, :, None]).astype(i32), axis=2)
    groups = holders // hold
    request_ids = jnp.arange(requests, dtype=i32)
    earlier = request_ids[None, :] < request_ids[:, None]

    def before(sent):
        return jnp.sum((earlier[:, :, None] & sent[None, :, :]).astype(i32), axis=1)

    places = pages // holders
    came = (rank % groups == me // hold) & (count > me % hold)
    came_turn = before(came)

    def pass_table(turn):
        place = rank // groups
        chosen = (
            came[:, :, None]
            & (place[:, :, None] == jnp.arange(places, dtype=i32)[None, None, :])
            & (came_turn // CAP == turn)[:, :, None]
        )
        origin = ids[None, :] * CAP + came_turn % CAP + 1
        return (jnp.sum(jnp.where(chosen, origin[:, :, None], 0), axis=1) - 1).reshape(-1)

    all_to = (rank[:, :, None] % groups == ids[None, None, :] // hold) & (
        count[:, :, None] > ids[None, None, :] % hold
    )
    rounds = (jnp.max(jnp.sum(all_to.astype(i32), axis=0)) + CAP - 1) // CAP

    own_holder = lax.dynamic_slice_in_dim(holder_of, me, 1, 0)[0]
    own_rank = lax.dynamic_slice_in_dim(rank, me, 1, 0)[0]
    page_rank = jnp.sum(
        jnp.where(own_holder[:, None] == ids[None, :], own_rank[None, :], 0), axis=1
    )
    page_nth = jnp.sum(
        (
            (page_ids[None, :] < page_ids[:, None])
            & (own_holder[None, :] == own_holder[:, None])
        ).astype(i32),
        axis=1,
    )
    unit = page_rank * hold + page_nth
    found = jnp.where(own_holder >= 0, (unit % holders) * places + unit // holders, 0)
    return pass_table, rounds, found


def staged(total, group, load, stage, packed, got_sem, put_sem):
    for g in range(total // group):
        for i in range(g * group, (g + 1) * group):
            load(i, got_sem.at[g])
    for g in range(total // group):
        part = pl.ds(g * group, group)
        pltpu.make_async_copy(stage.at[part], stage.at[part], got_sem.at[g]).wait()
        pltpu.make_async_copy(stage.at[part], packed.at[part], put_sem).start()
    pltpu.make_async_copy(stage, packed, put_sem).wait()


def pack_kernel(
    where_and_turn, page_table, keys, values, packed, table_v, table, stage, table_sem, got_sem, put_sem
):
    me, turn = where_and_turn[0], where_and_turn[1]
    requests, pages = page_table.shape
    slots = keys.shape[0]
    holders = packed.shape[0] // CAP
    groups = holders // HOLD
    i32 = jnp.int32
    slot_of = page_table[...]
    holder_of = jnp.where(slot_of >= 0, slot_of // slots, -1)
    local = slot_of % slots
    page_ids = lax.broadcasted_iota(i32, slot_of.shape, 1)
    mine = holder_of == me

    def first_of(on):
        return jnp.min(jnp.where(on, page_ids, pages), axis=1, keepdims=True)

    own_first = first_of(mine)
    rank = jnp.zeros((requests, 1), i32)
    for holder in range(holders):
        rank += (first_of(holder_of == holder) < own_first).astype(i32)
    mine_f = mine.astype(F32)
    count = jnp.sum(mine_f, axis=1, keepdims=True).astype(i32)
    before = lax.broadcasted_iota(i32, (pages, pages), 0) < lax.broadcasted_iota(
        i32, (pages, pages), 1
    )
    nth = jnp.dot(mine_f, before.astype(F32), preferred_element_type=F32).astype(i32)
    target = lax.broadcasted_iota(i32, (requests, holders), 1)
    to = (rank % groups == target // HOLD) & (count > target % HOLD)
    source = jnp.zeros((requests, holders), i32)
    for k in range(HOLD):
        hit = jnp.sum(jnp.where(mine & (nth == k), local, 0), axis=1, keepdims=True)
        source = jnp.where(target % HOLD == k, hit, source)
    earlier = lax.broadcasted_iota(i32, (requests, requests), 1) < lax.broadcasted_iota(
        i32, (requests, requests), 0
    )
    order = jnp.dot(
        earlier.astype(F32), to.astype(F32), preferred_element_type=F32
    ).astype(i32)
    for place in range(CAP):
        chosen = to & (order == turn * CAP + place)
        table_v[place : place + 1, 0:holders] = jnp.sum(
            jnp.where(chosen, source, 0), axis=0, keepdims=True
        )
    copy = pltpu.make_async_copy(table_v, table, table_sem)
    copy.start()
    copy.wait()

    def load(i, sem):
        slot = table[i % CAP, i // CAP]
        pltpu.make_async_copy(keys.at[slot], stage.at[i, 0], sem).start()
        pltpu.make_async_copy(values.at[slot], stage.at[i, 1], sem).start()

    staged(stage.shape[0], GROUP, load, stage, packed, got_sem, put_sem)


def repack_kernel(table, got, packed, stage, got_sem, put_sem):
    def load(i, sem):
        pltpu.make_async_copy(got.at[jnp.maximum(table[i], 0)], stage.at[i], sem).start()

    staged(stage.shape[0], GROUP, load, stage, packed, got_sem, put_sem)


def staging(shape):
    return [
        pltpu.VMEM(shape, BF16),
        pltpu.SemaphoreType.DMA((shape[0] // GROUP,)),
        pltpu.SemaphoreType.DMA,
    ]


def pack_pages(me, turn, page_table, keys, values):
    shape = (lax.axis_size("pages") * CAP, 2) + keys.shape[1:]
    return pl.pallas_call(
        pack_kernel,
        out_shape=jax.ShapeDtypeStruct(shape, BF16),
        in_specs=[SMEM, VMEM, ANY, ANY],
        out_specs=ANY,
        scratch_shapes=[
            pltpu.VMEM((8, 128), jnp.int32),
            pltpu.SMEM((8, 128), jnp.int32),
            staging(shape)[0],
            pltpu.SemaphoreType.DMA,
        ]
        + staging(shape)[1:],
        compiler_params=pltpu.CompilerParams(vmem_limit_bytes=60 << 20),
        name="pack_pages",
    )(jnp.stack([me, turn]).astype(jnp.int32), page_table, keys, values)


def repack_pages(table, got):
    return pl.pallas_call(
        repack_kernel,
        out_shape=jax.ShapeDtypeStruct(got.shape, BF16),
        in_specs=[SMEM, ANY],
        out_specs=ANY,
        scratch_shapes=staging(got.shape),
        compiler_params=pltpu.CompilerParams(vmem_limit_bytes=60 << 20),
        name="repack_pages",
    )(table, got)


def exchange(pages):
    holders = lax.axis_size("pages")
    shape = pages.shape
    sent = lax.all_to_all(
        pages.reshape((holders, shape[0] // holders) + shape[1:]), "pages", 0, 0, tiled=True
    )
    return sent.reshape(shape)


def pages_to_owners(page_table, keys, values, later):
    holders = lax.axis_size("pages")
    me = lax.axis_index("pages")
    packed, table, later = lax.optimization_barrier(
        (pack_pages(me, 0, page_table, keys, values), page_table, later)
    )
    pass_table, rounds, found = routing(table, me, holders, keys.shape[0], HOLD)
    x_parts = lax.all_gather(later[0], "mlp", axis=0)
    first, x_parts = lax.optimization_barrier((exchange(packed), x_parts))
    middle = repack_pages(pass_table(0), first)

    def further(turn, middle):
        got = exchange(pack_pages(me, turn, page_table, keys, values))
        table = pass_table(turn)
        return jnp.where((table >= 0)[:, None, None, None], repack_pages(table, got), middle)

    middle = lax.fori_loop(1, rounds, further, middle)
    return exchange(middle), found, x_parts, later[1:]


def two_heads(rows):
    lane = lax.broadcasted_iota(jnp.int32, rows.shape, 1)
    low = jnp.where(lane < HD, rows, 0.0)
    high = jnp.where(lane < HD, 0.0, rows)
    return jnp.concatenate([low, high], axis=0).astype(BF16)


def project_kernel(x_ref, wq, wk, wv, wg, queries, global_rows, key_rows, value_rows, x_all):
    shards, _, width = x_ref.shape
    for i in range(shards):
        x_all[:, i * width : (i + 1) * width] = x_ref[i]
    x = x_all[...]

    def project(matrix):
        return jnp.dot(x, matrix[...], preferred_element_type=F32).astype(BF16)

    scale = HD ** (-0.5)
    queries[...] = two_heads(project(wq).astype(F32) * scale)
    global_rows[...] = two_heads(project(wg).astype(F32) * scale)
    key_rows[...] = project(wk)
    value_rows[...] = project(wv)


def project_all(x_parts, wq, wk, wv, wg):
    shards, rows, width = x_parts.shape
    doubled = jax.ShapeDtypeStruct((2 * rows, width), BF16)
    single = jax.ShapeDtypeStruct((rows, width), BF16)
    return pl.pallas_call(
        project_kernel,
        out_shape=(doubled, doubled, single, single),
        in_specs=[VMEM] * 5,
        out_specs=(VMEM,) * 4,
        scratch_shapes=[pltpu.VMEM((rows, shards * width), BF16)],
        name="project",
    )(x_parts, wq, wk, wv, wg)


def attention_kernel(inner, found, length, *refs):
    given = refs[: 5 if inner else 4]
    pages, out, key_buf, value_buf, kept, peak, acc, ksem, vsem = refs[len(given) :][:9]
    projected = refs[len(given) + 9 :]
    queries, global_rows, key_rows, value_rows = projected[:4] if inner else given
    per_block = KEY_BLOCK // PAGE
    shards, rows, width = out.shape
    limit = length[0]
    blocks = (limit + KEY_BLOCK - 1) // KEY_BLOCK

    def block_rows(block):
        return pl.ds(pl.multiple_of(block * KEY_BLOCK, KEY_BLOCK), KEY_BLOCK)

    def fetch(block, carry, part, buf, sem):
        for i in range(per_block):
            page = block * per_block + i
            rows = pl.ds(pl.multiple_of(page * PAGE, PAGE), PAGE)
            pltpu.make_async_copy(pages.at[found[page], part], buf.at[rows], sem.at[block]).start()
        return carry

    lax.fori_loop(0, blocks, functools.partial(fetch, part=0, buf=key_buf, sem=ksem), 0)
    lax.fori_loop(0, blocks, functools.partial(fetch, part=1, buf=value_buf, sem=vsem), 0)
    if inner:
        project_kernel(*given, *projected)
    def scores_of(left, keys):
        return lax.dot_general(
            left, keys, (((1,), (1,)), ((), ())), preferred_element_type=F32
        ) * LOG2E

    def fold(scores):
        parts = [scores[:, i : i + 128] for i in range(0, scores.shape[1], 128)]
        while len(parts) > 1:
            parts = [jnp.maximum(*parts[i : i + 2]) for i in range(0, len(parts), 2)]
        return parts[0]

    def weigh(scores, top, values):
        ones = jnp.ones(values.shape, BF16)
        weights = jnp.exp2(scores - top).astype(BF16)
        return jnp.dot(
            weights, jnp.concatenate([values, ones], axis=1), preferred_element_type=F32
        )

    own = scores_of(queries[...], key_rows[...])
    peak[...] = fold(own)

    def score_step(block, carry):
        part = key_buf.at[block_rows(block)]
        pltpu.make_async_copy(part, part, ksem.at[block]).wait()
        scores = scores_of(global_rows[...], key_buf[block_rows(block), :])
        position = block * KEY_BLOCK + lax.broadcasted_iota(jnp.int32, scores.shape, 1)
        scores = jnp.where(position < limit, scores, NEG)
        kept[block] = scores
        peak[...] = jnp.maximum(peak[...], fold(scores))
        return carry

    lax.fori_loop(0, blocks, score_step, 0)
    top = jnp.max(peak[...], axis=1, keepdims=True)
    peak[...] = jnp.broadcast_to(top, peak.shape)
    acc[...] = weigh(own, top, value_rows[...])

    def weigh_step(block, carry):
        part = value_buf.at[block_rows(block)]
        pltpu.make_async_copy(part, part, vsem.at[block]).wait()
        acc[...] += weigh(kept[block], peak[:, :1], value_buf[block_rows(block), :])
        return carry

    lax.fori_loop(0, blocks, weigh_step, 0)
    total = acc[...]
    ratio = total[:, :width] / total[:, width:]
    lane = lax.broadcasted_iota(jnp.int32, (rows, width), 1)
    result = jnp.where(lane < HD, ratio[:rows], ratio[rows:]).astype(BF16)
    for i in range(shards):
        out[i] = result


def attend(found, length, shards, given, pages):
    inner = len(given) == 5
    rows, width = given[0].shape[1:] if inner else given[2].shape
    longest = found.shape[0] * PAGE
    scratch = [
        pltpu.VMEM((longest, width), BF16),
        pltpu.VMEM((longest, width), BF16),
        pltpu.VMEM((longest // KEY_BLOCK, 2 * rows, KEY_BLOCK), F32),
        pltpu.VMEM((2 * rows, 128), F32),
        pltpu.VMEM((2 * rows, 2 * width), F32),
        pltpu.SemaphoreType.DMA((longest // KEY_BLOCK,)),
        pltpu.SemaphoreType.DMA((longest // KEY_BLOCK,)),
    ]
    if inner:
        scratch += [
            pltpu.VMEM((2 * rows, width), BF16),
            pltpu.VMEM((2 * rows, width), BF16),
            pltpu.VMEM((rows, width), BF16),
            pltpu.VMEM((rows, width), BF16),
            pltpu.VMEM((rows, shards * width), BF16),
        ]
    return pl.pallas_call(
        functools.partial(attention_kernel, inner),
        out_shape=jax.ShapeDtypeStruct((shards, rows, width), BF16),
        in_specs=[SMEM, SMEM] + [VMEM] * len(given) + [ANY],
        out_specs=VMEM,
        scratch_shapes=scratch,
        compiler_params=pltpu.CompilerParams(vmem_limit_bytes=56 << 20),
        name="attention",
    )(found, length, *given, pages)


def normalize(total, gain, bias, width):
    mean = jnp.sum(total, axis=1, keepdims=True) * (1.0 / width)
    square = jnp.sum(total * total, axis=1, keepdims=True) * (1.0 / width)
    inverse = lax.rsqrt(square - mean * mean + EPS)
    return ((total - mean) * inverse * gain + bias).astype(BF16)


def ffn_kernel(
    place,
    att,
    x_ref,
    accept,
    low_a,
    low_b,
    up_a,
    up_b,
    down_a,
    down_b,
    g1,
    b1,
    g2,
    b2,
    out,
    wide,
    hidden,
    acc,
    w_out,
    w_sem,
):
    step = pl.program_id(0)
    shards, rows, width = x_ref.shape
    full = shards * width
    column, core = place[0], place[1]

    @pl.when(step == 0)
    def _():
        half = width // 2
        skip = down_a.shape[1]
        for i in range(shards):
            for low, owner in ((low_a, core), (low_b, 1 - core)):
                at = pl.ds(pl.multiple_of(i * width + owner * half, half), half)
                pltpu.make_async_copy(low.at[i, skip : skip + half], w_out.at[at], w_sem).start()
        for i in range(shards):
            wide[:, i * width : (i + 1) * width] = att[i]
        pltpu.make_async_copy(w_out, w_out, w_sem).wait()
        total = jnp.dot(wide[...], w_out[...], preferred_element_type=F32)
        for i in range(shards):
            wide[:, i * width : (i + 1) * width] = x_ref[i]
        total = total + wide[...].astype(F32)
        hidden[...] = normalize(total, g1[...], b1[...], full)
        acc[...] = hidden[...].astype(F32)

    h = hidden[...]
    raised = [
        jnp.dot(h, up[i], preferred_element_type=F32)
        for i in range(up_a.shape[0])
        for up in (up_a, up_b)
    ]
    active = [(0.5 * v * (1.0 + lax.erf(v * (0.5**0.5)))).astype(BF16) for v in raised]
    downs = [down[i] for i in range(up_a.shape[0]) for down in (down_a, down_b)]
    acc[...] += jnp.dot(
        jnp.concatenate(active, axis=1),
        jnp.concatenate(downs, axis=0),
        preferred_element_type=F32,
    )

    @pl.when(step == pl.num_programs(0) - 1)
    def _():
        result = normalize(acc[...], g2[...], b2[...], full)
        chosen = accept[...] != 0
        if out.shape[0] == shards:
            for i in range(shards):
                out[i] = jnp.where(chosen, result[:, i * width : (i + 1) * width], x_ref[i])
        else:
            for i in range(shards):

                @pl.when(column == i)
                def _():
                    out[0] = jnp.where(chosen, result[:, i * width : (i + 1) * width], x_ref[i])


def feed_forward(place, outs, att, x_parts, accept, up, low, g1, b1, g2, b2):
    shards, rows, width = x_parts.shape
    full = shards * width
    units = up[0].shape[2]

    def fixed(shape):
        return pl.BlockSpec(shape, lambda i: (0,) * len(shape), pipeline_mode=pl.Buffered(1))

    def part(*shape):
        return pl.BlockSpec((PER,) + shape, lambda i: (i, 0, 0))

    return pl.pallas_call(
        ffn_kernel,
        grid=(shards // PER,),
        out_shape=jax.ShapeDtypeStruct((outs, rows, width), BF16),
        in_specs=[SMEM, fixed(x_parts.shape), fixed(x_parts.shape), fixed((rows, 1)), ANY, ANY]
        + [part(full, units)] * 2
        + [part(units, full)] * 2
        + [fixed((1, full))] * 4,
        out_specs=pl.BlockSpec((outs, rows, width), lambda i: (0, 0, 0)),
        scratch_shapes=[
            pltpu.VMEM((rows, full), BF16),
            pltpu.VMEM((rows, full), BF16),
            pltpu.VMEM((rows, full), F32),
            pltpu.VMEM((full, full), BF16),
            pltpu.SemaphoreType.DMA,
        ],
        compiler_params=pltpu.CompilerParams(
            dimension_semantics=("arbitrary",), vmem_limit_bytes=60 << 20
        ),
        name="feed_forward",
    )(place, att, x_parts, accept, *low, *up, *low, g1, b1, g2, b2)


def to_all(copies):
    return lax.all_to_all(copies, "mlp", 0, 0, tiled=True)


def core_pair():
    return [(i, i ^ 1) for i in range(lax.axis_size("pages"))]


def per_device(
    embeddings,
    w_query,
    w_key,
    w_value,
    w_global_query,
    w_out,
    w_up,
    w_down,
    norm1_gain,
    norm1_bias,
    norm2_gain,
    norm2_bias,
    cache_keys,
    cache_values,
    lengths,
    page_table,
    accept,
):
    shards = lax.axis_size("mlp")
    me = lax.axis_index("pages")
    shard = lax.axis_index("mlp")
    rows, width = embeddings.shape
    pages, found, x_parts, (w_up, w_down, w_out) = pages_to_owners(
        page_table, cache_keys, cache_values, (embeddings, w_up, w_down, w_out)
    )
    length = lax.dynamic_slice_in_dim(lengths, me, 1, 0)

    core = me % 2
    half = w_up.shape[1] // 2
    half_out = w_out.shape[0] // 2
    up_half = lax.dynamic_slice_in_dim(w_up, core * half, half, 1)
    down_half = lax.dynamic_slice_in_dim(w_down, core * half, half, 0)
    out_half = lax.dynamic_slice_in_dim(w_out, core * half_out, half_out, 0)
    up_mine = lax.all_gather(up_half, "mlp", axis=0)
    low_mine = lax.all_gather(jnp.concatenate([down_half, out_half]), "mlp", axis=0)
    norms = [v.reshape(1, -1) for v in (norm1_gain, norm1_bias, norm2_gain, norm2_bias)]
    place = jnp.stack([shard, core]).astype(jnp.int32)
    projections = (w_query, w_key, w_value, w_global_query)

    def layer(outs, attention, x_parts, taken, up, low):
        return feed_forward(
            place, outs, to_all(attention), x_parts, taken.reshape(rows, 1), up, low, *norms
        )

    attention = attend(found, length, shards, project_all(x_parts, *projections), pages)
    attention, low_mine = lax.optimization_barrier((attention, low_mine))
    up = (up_mine, lax.ppermute(up_mine, "pages", core_pair()))
    low = (low_mine, lax.ppermute(low_mine, "pages", core_pair()))
    middle = layer(shards, attention, x_parts, accept[0], up, low)
    attention = attend(found, length, shards, (middle,) + projections, pages)
    return layer(1, attention, middle, accept[1], up, low).reshape(rows, width)


def solution(mesh):
    return jax.shard_map(
        per_device,
        mesh=mesh,
        in_specs=(
            P("pages", "mlp"),
            P(None, "mlp"),
            P(None, "mlp"),
            P(None, "mlp"),
            P(None, "mlp"),
            P("mlp", None),
            P(None, "mlp"),
            P("mlp", None),
            P(),
            P(),
            P(),
            P(),
            P("pages", None, "mlp"),
            P("pages", None, "mlp"),
            P(),
            P(),
            P(None, "pages"),
        ),
        out_specs=P("pages", "mlp"),
        check_vma=False,
    )
```

```python
import functools

import jax
import jax.numpy as jnp
from jax import lax
from jax.experimental import pallas as pl
from jax.experimental.pallas import tpu as pltpu
from jax.sharding import PartitionSpec as P

HD = 64
BLK = 256
PAGE = 128
EPS = 1e-05
NEG = -1e30
CAP = 2
KEY_BLOCK = 4096
GROUP = 8
HOLD = 8
PER = 2
LOG2E = 1.4426950408889634
F32 = jnp.float32
BF16 = jnp.bfloat16
VMEM = pl.BlockSpec(memory_space=pltpu.VMEM)
ANY = pl.BlockSpec(memory_space=pl.ANY)
SMEM = pl.BlockSpec(memory_space=pltpu.SMEM)


def routing(page_table, me, holders, slots, hold):
    requests, pages = page_table.shape
    i32 = jnp.int32
    holder_of = jnp.where(page_table >= 0, page_table // slots, -1)
    ids = jnp.arange(holders, dtype=i32)
    page_ids = jnp.arange(pages, dtype=i32)
    on = holder_of[:, None, :] == ids[None, :, None]
    first = jnp.min(jnp.where(on, page_ids[None, None, :], pages), axis=2)
    count = jnp.sum(on.astype(i32), axis=2)
    rank = jnp.sum((first[:, None, :] < first[:, :, None]).astype(i32), axis=2)
    groups = holders // hold
    request_ids = jnp.arange(requests, dtype=i32)
    earlier = request_ids[None, :] < request_ids[:, None]

    def before(sent):
        return jnp.sum((earlier[:, :, None] & sent[None, :, :]).astype(i32), axis=1)

    places = pages // holders
    came = (rank % groups == me // hold) & (count > me % hold)
    came_turn = before(came)

    def pass_table(turn):
        place = rank // groups
        chosen = (
            came[:, :, None]
            & (place[:, :, None] == jnp.arange(places, dtype=i32)[None, None, :])
            & (came_turn // CAP == turn)[:, :, None]
        )
        origin = ids[None, :] * CAP + came_turn % CAP + 1
        return (jnp.sum(jnp.where(chosen, origin[:, :, None], 0), axis=1) - 1).reshape(-1)

    all_to = (rank[:, :, None] % groups == ids[None, None, :] // hold) & (
        count[:, :, None] > ids[None, None, :] % hold
    )
    rounds = (jnp.max(jnp.sum(all_to.astype(i32), axis=0)) + CAP - 1) // CAP

    own_holder = lax.dynamic_slice_in_dim(holder_of, me, 1, 0)[0]
    own_rank = lax.dynamic_slice_in_dim(rank, me, 1, 0)[0]
    page_rank = jnp.sum(
        jnp.where(own_holder[:, None] == ids[None, :], own_rank[None, :], 0), axis=1
    )
    page_nth = jnp.sum(
        (
            (page_ids[None, :] < page_ids[:, None])
            & (own_holder[None, :] == own_holder[:, None])
        ).astype(i32),
        axis=1,
    )
    unit = page_rank * hold + page_nth
    found = jnp.where(own_holder >= 0, (unit % holders) * places + unit // holders, 0)
    return pass_table, rounds, found


def staged(total, group, load, stage, packed, got_sem, put_sem):
    for g in range(total // group):
        for i in range(g * group, (g + 1) * group):
            load(i, got_sem.at[g])
    for g in range(total // group):
        part = pl.ds(g * group, group)
        pltpu.make_async_copy(stage.at[part], stage.at[part], got_sem.at[g]).wait()
        pltpu.make_async_copy(stage.at[part], packed.at[part], put_sem).start()
    pltpu.make_async_copy(stage, packed, put_sem).wait()


def pack_kernel(
    where_and_turn, page_table, keys, values, packed, table_v, table, stage, table_sem, got_sem, put_sem
):
    me, turn = where_and_turn[0], where_and_turn[1]
    requests, pages = page_table.shape
    slots = keys.shape[0]
    holders = packed.shape[0] // CAP
    groups = holders // HOLD
    i32 = jnp.int32
    slot_of = page_table[...]
    holder_of = jnp.where(slot_of >= 0, slot_of // slots, -1)
    local = slot_of % slots
    page_ids = lax.broadcasted_iota(i32, slot_of.shape, 1)
    mine = holder_of == me

    def first_of(on):
        return jnp.min(jnp.where(on, page_ids, pages), axis=1, keepdims=True)

    own_first = first_of(mine)
    rank = jnp.zeros((requests, 1), i32)
    for holder in range(holders):
        rank += (first_of(holder_of == holder) < own_first).astype(i32)
    mine_f = mine.astype(F32)
    count = jnp.sum(mine_f, axis=1, keepdims=True).astype(i32)
    before = lax.broadcasted_iota(i32, (pages, pages), 0) < lax.broadcasted_iota(
        i32, (pages, pages), 1
    )
    nth = jnp.dot(mine_f, before.astype(F32), preferred_element_type=F32).astype(i32)
    target = lax.broadcasted_iota(i32, (requests, holders), 1)
    to = (rank % groups == target // HOLD) & (count > target % HOLD)
    source = jnp.zeros((requests, holders), i32)
    for k in range(HOLD):
        hit = jnp.sum(jnp.where(mine & (nth == k), local, 0), axis=1, keepdims=True)
        source = jnp.where(target % HOLD == k, hit, source)
    earlier = lax.broadcasted_iota(i32, (requests, requests), 1) < lax.broadcasted_iota(
        i32, (requests, requests), 0
    )
    order = jnp.dot(
        earlier.astype(F32), to.astype(F32), preferred_element_type=F32
    ).astype(i32)
    for place in range(CAP):
        chosen = to & (order == turn * CAP + place)
        table_v[place : place + 1, 0:holders] = jnp.sum(
            jnp.where(chosen, source, 0), axis=0, keepdims=True
        )
    copy = pltpu.make_async_copy(table_v, table, table_sem)
    copy.start()
    copy.wait()

    def load(i, sem):
        slot = table[i % CAP, i // CAP]
        pltpu.make_async_copy(keys.at[slot], stage.at[i, 0], sem).start()
        pltpu.make_async_copy(values.at[slot], stage.at[i, 1], sem).start()

    staged(stage.shape[0], GROUP, load, stage, packed, got_sem, put_sem)


def repack_kernel(table, got, packed, stage, got_sem, put_sem):
    def load(i, sem):
        pltpu.make_async_copy(got.at[jnp.maximum(table[i], 0)], stage.at[i], sem).start()

    staged(stage.shape[0], GROUP, load, stage, packed, got_sem, put_sem)


def staging(shape):
    return [
        pltpu.VMEM(shape, BF16),
        pltpu.SemaphoreType.DMA((shape[0] // GROUP,)),
        pltpu.SemaphoreType.DMA,
    ]


def pack_pages(me, turn, page_table, keys, values):
    shape = (lax.axis_size("pages") * CAP, 2) + keys.shape[1:]
    return pl.pallas_call(
        pack_kernel,
        out_shape=jax.ShapeDtypeStruct(shape, BF16),
        in_specs=[SMEM, VMEM, ANY, ANY],
        out_specs=ANY,
        scratch_shapes=[
            pltpu.VMEM((8, 128), jnp.int32),
            pltpu.SMEM((8, 128), jnp.int32),
            staging(shape)[0],
            pltpu.SemaphoreType.DMA,
        ]
        + staging(shape)[1:],
        compiler_params=pltpu.CompilerParams(vmem_limit_bytes=60 << 20),
        name="pack_pages",
    )(jnp.stack([me, turn]).astype(jnp.int32), page_table, keys, values)


def repack_pages(table, got):
    return pl.pallas_call(
        repack_kernel,
        out_shape=jax.ShapeDtypeStruct(got.shape, BF16),
        in_specs=[SMEM, ANY],
        out_specs=ANY,
        scratch_shapes=staging(got.shape),
        compiler_params=pltpu.CompilerParams(vmem_limit_bytes=60 << 20),
        name="repack_pages",
    )(table, got)


def exchange(pages):
    holders = lax.axis_size("pages")
    shape = pages.shape
    sent = lax.all_to_all(
        pages.reshape((holders, shape[0] // holders) + shape[1:]), "pages", 0, 0, tiled=True
    )
    return sent.reshape(shape)


def pages_to_owners(page_table, keys, values, later):
    holders = lax.axis_size("pages")
    me = lax.axis_index("pages")
    packed, table, later = lax.optimization_barrier(
        (pack_pages(me, 0, page_table, keys, values), page_table, later)
    )
    pass_table, rounds, found = routing(table, me, holders, keys.shape[0], HOLD)
    x_parts = lax.all_gather(later[0], "mlp", axis=0)
    first, x_parts = lax.optimization_barrier((exchange(packed), x_parts))
    middle = repack_pages(pass_table(0), first)

    def further(turn, middle):
        got = exchange(pack_pages(me, turn, page_table, keys, values))
        table = pass_table(turn)
        return jnp.where((table >= 0)[:, None, None, None], repack_pages(table, got), middle)

    middle = lax.fori_loop(1, rounds, further, middle)
    return exchange(middle), found, x_parts, later[1:]


def two_heads(rows):
    lane = lax.broadcasted_iota(jnp.int32, rows.shape, 1)
    low = jnp.where(lane < HD, rows, 0.0)
    high = jnp.where(lane < HD, 0.0, rows)
    return jnp.concatenate([low, high], axis=0).astype(BF16)


def project_kernel(x_ref, wq, wk, wv, wg, queries, global_rows, key_rows, value_rows, x_all):
    shards, _, width = x_ref.shape
    for i in range(shards):
        x_all[:, i * width : (i + 1) * width] = x_ref[i]
    x = x_all[...]

    def project(matrix):
        return jnp.dot(x, matrix[...], preferred_element_type=F32).astype(BF16)

    scale = HD ** (-0.5)
    queries[...] = two_heads(project(wq).astype(F32) * scale)
    global_rows[...] = two_heads(project(wg).astype(F32) * scale)
    key_rows[...] = project(wk)
    value_rows[...] = project(wv)


def project_all(x_parts, wq, wk, wv, wg):
    shards, rows, width = x_parts.shape
    doubled = jax.ShapeDtypeStruct((2 * rows, width), BF16)
    single = jax.ShapeDtypeStruct((rows, width), BF16)
    return pl.pallas_call(
        project_kernel,
        out_shape=(doubled, doubled, single, single),
        in_specs=[VMEM] * 5,
        out_specs=(VMEM,) * 4,
        scratch_shapes=[pltpu.VMEM((rows, shards * width), BF16)],
        name="project",
    )(x_parts, wq, wk, wv, wg)


def attention_kernel(inner, found, length, *refs):
    given = refs[: 5 if inner else 4]
    pages, out, key_buf, value_buf, kept, peak, acc, ksem, vsem = refs[len(given) :][:9]
    projected = refs[len(given) + 9 :]
    queries, global_rows, key_rows, value_rows = projected[:4] if inner else given
    per_block = KEY_BLOCK // PAGE
    shards, rows, width = out.shape
    limit = length[0]
    blocks = (limit + KEY_BLOCK - 1) // KEY_BLOCK

    def block_rows(block):
        return pl.ds(pl.multiple_of(block * KEY_BLOCK, KEY_BLOCK), KEY_BLOCK)

    def fetch(block, carry, part, buf, sem):
        for i in range(per_block):
            page = block * per_block + i
            rows = pl.ds(pl.multiple_of(page * PAGE, PAGE), PAGE)
            pltpu.make_async_copy(pages.at[found[page], part], buf.at[rows], sem.at[block]).start()
        return carry

    lax.fori_loop(0, blocks, functools.partial(fetch, part=0, buf=key_buf, sem=ksem), 0)
    lax.fori_loop(0, blocks, functools.partial(fetch, part=1, buf=value_buf, sem=vsem), 0)
    if inner:
        project_kernel(*given, *projected)
    def scores_of(left, keys):
        return lax.dot_general(
            left, keys, (((1,), (1,)), ((), ())), preferred_element_type=F32
        ) * LOG2E

    def fold(scores):
        parts = [scores[:, i : i + 128] for i in range(0, scores.shape[1], 128)]
        while len(parts) > 1:
            parts = [jnp.maximum(*parts[i : i + 2]) for i in range(0, len(parts), 2)]
        return parts[0]

    def weigh(scores, top, values):
        ones = jnp.ones(values.shape, BF16)
        weights = jnp.exp2(scores - top).astype(BF16)
        return jnp.dot(
            weights, jnp.concatenate([values, ones], axis=1), preferred_element_type=F32
        )

    own = scores_of(queries[...], key_rows[...])
    peak[...] = fold(own)

    def score_step(block, carry):
        part = key_buf.at[block_rows(block)]
        pltpu.make_async_copy(part, part, ksem.at[block]).wait()
        scores = scores_of(global_rows[...], key_buf[block_rows(block), :])
        position = block * KEY_BLOCK + lax.broadcasted_iota(jnp.int32, scores.shape, 1)
        scores = jnp.where(position < limit, scores, NEG)
        kept[block] = scores
        peak[...] = jnp.maximum(peak[...], fold(scores))
        return carry

    lax.fori_loop(0, blocks, score_step, 0)
    top = jnp.max(peak[...], axis=1, keepdims=True)
    peak[...] = jnp.broadcast_to(top, peak.shape)
    acc[...] = weigh(own, top, value_rows[...])

    def weigh_step(block, carry):
        part = value_buf.at[block_rows(block)]
        pltpu.make_async_copy(part, part, vsem.at[block]).wait()
        acc[...] += weigh(kept[block], peak[:, :1], value_buf[block_rows(block), :])
        return carry

    lax.fori_loop(0, blocks, weigh_step, 0)
    total = acc[...]
    ratio = total[:, :width] / total[:, width:]
    lane = lax.broadcasted_iota(jnp.int32, (rows, width), 1)
    result = jnp.where(lane < HD, ratio[:rows], ratio[rows:]).astype(BF16)
    for i in range(shards):
        out[i] = result


def attend(found, length, shards, given, pages):
    inner = len(given) == 5
    rows, width = given[0].shape[1:] if inner else given[2].shape
    longest = found.shape[0] * PAGE
    scratch = [
        pltpu.VMEM((longest, width), BF16),
        pltpu.VMEM((longest, width), BF16),
        pltpu.VMEM((longest // KEY_BLOCK, 2 * rows, KEY_BLOCK), F32),
        pltpu.VMEM((2 * rows, 128), F32),
        pltpu.VMEM((2 * rows, 2 * width), F32),
        pltpu.SemaphoreType.DMA((longest // KEY_BLOCK,)),
        pltpu.SemaphoreType.DMA((longest // KEY_BLOCK,)),
    ]
    if inner:
        scratch += [
            pltpu.VMEM((2 * rows, width), BF16),
            pltpu.VMEM((2 * rows, width), BF16),
            pltpu.VMEM((rows, width), BF16),
            pltpu.VMEM((rows, width), BF16),
            pltpu.VMEM((rows, shards * width), BF16),
        ]
    return pl.pallas_call(
        functools.partial(attention_kernel, inner),
        out_shape=jax.ShapeDtypeStruct((shards, rows, width), BF16),
        in_specs=[SMEM, SMEM] + [VMEM] * len(given) + [ANY],
        out_specs=VMEM,
        scratch_shapes=scratch,
        compiler_params=pltpu.CompilerParams(vmem_limit_bytes=56 << 20),
        name="attention",
    )(found, length, *given, pages)


def normalize(total, gain, bias, width):
    mean = jnp.sum(total, axis=1, keepdims=True) * (1.0 / width)
    square = jnp.sum(total * total, axis=1, keepdims=True) * (1.0 / width)
    inverse = lax.rsqrt(square - mean * mean + EPS)
    return ((total - mean) * inverse * gain + bias).astype(BF16)


def ffn_kernel(
    place,
    att,
    x_in,
    accept,
    low_a,
    low_b,
    up_a,
    up_b,
    down_a,
    down_b,
    g1,
    b1,
    g2,
    b2,
    out,
    wide,
    hidden,
    acc,
    w_out,
    x_ref,
    w_sem,
    a_sem,
    x_sem,
):
    step = pl.program_id(0)
    shards, rows, width = x_ref.shape
    full = shards * width
    column, core = place[0], place[1]

    @pl.when(step == 0)
    def _():
        pltpu.make_async_copy(x_in, x_ref, x_sem).start()
        half = width // 2
        skip = down_a.shape[1]
        for i in range(shards):
            for low, owner in ((low_a, core), (low_b, 1 - core)):
                at = pl.ds(pl.multiple_of(i * width + owner * half, half), half)
                pltpu.make_async_copy(low.at[i, skip : skip + half], w_out.at[at], w_sem).start()
            pltpu.make_async_copy(att.at[i], wide.at[:, i * width : (i + 1) * width], a_sem).start()
        pltpu.make_async_copy(wide, wide, a_sem).wait()
        pltpu.make_async_copy(w_out, w_out, w_sem).wait()
        total = jnp.dot(wide[...], w_out[...], preferred_element_type=F32)
        pltpu.make_async_copy(x_in, x_ref, x_sem).wait()
        for i in range(shards):
            wide[:, i * width : (i + 1) * width] = x_ref[i]
        total = total + wide[...].astype(F32)
        hidden[...] = normalize(total, g1[...], b1[...], full)
        acc[...] = hidden[...].astype(F32)

    h = hidden[...]
    raised = [
        jnp.dot(h, up[i], preferred_element_type=F32)
        for i in range(up_a.shape[0])
        for up in (up_a, up_b)
    ]
    active = [(0.5 * v * (1.0 + lax.erf(v * (0.5**0.5)))).astype(BF16) for v in raised]
    downs = [down[i] for i in range(up_a.shape[0]) for down in (down_a, down_b)]
    acc[...] += jnp.dot(
        jnp.concatenate(active, axis=1),
        jnp.concatenate(downs, axis=0),
        preferred_element_type=F32,
    )

    @pl.when(step == pl.num_programs(0) - 1)
    def _():
        result = normalize(acc[...], g2[...], b2[...], full)
        chosen = accept[...] != 0
        if out.shape[0] == shards:
            for i in range(shards):
                out[i] = jnp.where(chosen, result[:, i * width : (i + 1) * width], x_ref[i])
        else:
            for i in range(shards):

                @pl.when(column == i)
                def _():
                    out[0] = jnp.where(chosen, result[:, i * width : (i + 1) * width], x_ref[i])


def feed_forward(place, outs, att, x_parts, accept, up, low, g1, b1, g2, b2):
    shards, rows, width = x_parts.shape
    full = shards * width
    units = up[0].shape[2]

    def fixed(shape):
        return pl.BlockSpec(shape, lambda i: (0,) * len(shape), pipeline_mode=pl.Buffered(1))

    def part(*shape):
        return pl.BlockSpec((PER,) + shape, lambda i: (i, 0, 0))

    return pl.pallas_call(
        ffn_kernel,
        grid=(shards // PER,),
        out_shape=jax.ShapeDtypeStruct((outs, rows, width), BF16),
        in_specs=[SMEM, ANY, ANY, fixed((rows, 1)), ANY, ANY]
        + [part(full, units)] * 2
        + [part(units, full)] * 2
        + [fixed((1, full))] * 4,
        out_specs=pl.BlockSpec((outs, rows, width), lambda i: (0, 0, 0)),
        scratch_shapes=[
            pltpu.VMEM((rows, full), BF16),
            pltpu.VMEM((rows, full), BF16),
            pltpu.VMEM((rows, full), F32),
            pltpu.VMEM((full, full), BF16),
            pltpu.VMEM(x_parts.shape, BF16),
            pltpu.SemaphoreType.DMA,
            pltpu.SemaphoreType.DMA,
            pltpu.SemaphoreType.DMA,
        ],
        compiler_params=pltpu.CompilerParams(
            dimension_semantics=("arbitrary",), vmem_limit_bytes=60 << 20
        ),
        name="feed_forward",
    )(place, att, x_parts, accept, *low, *up, *low, g1, b1, g2, b2)


def to_all(copies):
    return lax.all_to_all(copies, "mlp", 0, 0, tiled=True)


def core_pair():
    return [(i, i ^ 1) for i in range(lax.axis_size("pages"))]


def per_device(
    embeddings,
    w_query,
    w_key,
    w_value,
    w_global_query,
    w_out,
    w_up,
    w_down,
    norm1_gain,
    norm1_bias,
    norm2_gain,
    norm2_bias,
    cache_keys,
    cache_values,
    lengths,
    page_table,
    accept,
):
    shards = lax.axis_size("mlp")
    me = lax.axis_index("pages")
    shard = lax.axis_index("mlp")
    rows, width = embeddings.shape
    pages, found, x_parts, (w_up, w_down, w_out) = pages_to_owners(
        page_table, cache_keys, cache_values, (embeddings, w_up, w_down, w_out)
    )
    length = lax.dynamic_slice_in_dim(lengths, me, 1, 0)

    core = me % 2
    half = w_up.shape[1] // 2
    half_out = w_out.shape[0] // 2
    up_half = lax.dynamic_slice_in_dim(w_up, core * half, half, 1)
    down_half = lax.dynamic_slice_in_dim(w_down, core * half, half, 0)
    out_half = lax.dynamic_slice_in_dim(w_out, core * half_out, half_out, 0)
    up_mine = lax.all_gather(up_half, "mlp", axis=0)
    low_mine = lax.all_gather(jnp.concatenate([down_half, out_half]), "mlp", axis=0)
    norms = [v.reshape(1, -1) for v in (norm1_gain, norm1_bias, norm2_gain, norm2_bias)]
    place = jnp.stack([shard, core]).astype(jnp.int32)
    projections = (w_query, w_key, w_value, w_global_query)

    def layer(outs, attention, x_parts, taken, up, low):
        return feed_forward(
            place, outs, to_all(attention), x_parts, taken.reshape(rows, 1), up, low, *norms
        )

    up = (up_mine, lax.ppermute(up_mine, "pages", core_pair()))
    pages, up = lax.optimization_barrier((pages, up))
    attention = attend(found, length, shards, project_all(x_parts, *projections), pages)
    attention, low_mine = lax.optimization_barrier((attention, low_mine))
    low = (low_mine, lax.ppermute(low_mine, "pages", core_pair()))
    middle = layer(shards, attention, x_parts, accept[0], up, low)
    attention = attend(found, length, shards, (middle,) + projections, pages)
    return layer(1, attention, middle, accept[1], up, low).reshape(rows, width)


def solution(mesh):
    return jax.shard_map(
        per_device,
        mesh=mesh,
        in_specs=(
            P("pages", "mlp"),
            P(None, "mlp"),
            P(None, "mlp"),
            P(None, "mlp"),
            P(None, "mlp"),
            P("mlp", None),
            P(None, "mlp"),
            P("mlp", None),
            P(),
            P(),
            P(),
            P(),
            P("pages", None, "mlp"),
            P("pages", None, "mlp"),
            P(),
            P(),
            P(None, "pages"),
        ),
        out_specs=P("pages", "mlp"),
        check_vma=False,
    )
```

```python
import functools

import jax
import jax.numpy as jnp
from jax import lax
from jax.experimental import pallas as pl
from jax.experimental.pallas import tpu as pltpu
from jax.sharding import PartitionSpec as P

HD = 64
BLK = 256
PAGE = 128
EPS = 1e-05
NEG = -1e30
CAP = 2
KEY_BLOCK = 4096
GROUP = 8
HOLD = 8
PER = 2
LOG2E = 1.4426950408889634
F32 = jnp.float32
BF16 = jnp.bfloat16
VMEM = pl.BlockSpec(memory_space=pltpu.VMEM)
ANY = pl.BlockSpec(memory_space=pl.ANY)
SMEM = pl.BlockSpec(memory_space=pltpu.SMEM)


def routing(page_table, me, holders, slots, hold):
    requests, pages = page_table.shape
    i32 = jnp.int32
    holder_of = jnp.where(page_table >= 0, page_table // slots, -1)
    ids = jnp.arange(holders, dtype=i32)
    page_ids = jnp.arange(pages, dtype=i32)
    on = holder_of[:, None, :] == ids[None, :, None]
    first = jnp.min(jnp.where(on, page_ids[None, None, :], pages), axis=2)
    count = jnp.sum(on.astype(i32), axis=2)
    rank = jnp.sum((first[:, None, :] < first[:, :, None]).astype(i32), axis=2)
    groups = holders // hold
    request_ids = jnp.arange(requests, dtype=i32)
    earlier = request_ids[None, :] < request_ids[:, None]

    def before(sent):
        return jnp.sum((earlier[:, :, None] & sent[None, :, :]).astype(i32), axis=1)

    places = pages // holders
    came = (rank % groups == me // hold) & (count > me % hold)
    came_turn = before(came)

    def pass_table(turn):
        place = rank // groups
        chosen = (
            came[:, :, None]
            & (place[:, :, None] == jnp.arange(places, dtype=i32)[None, None, :])
            & (came_turn // CAP == turn)[:, :, None]
        )
        origin = ids[None, :] * CAP + came_turn % CAP + 1
        return (jnp.sum(jnp.where(chosen, origin[:, :, None], 0), axis=1) - 1).reshape(-1)

    all_to = (rank[:, :, None] % groups == ids[None, None, :] // hold) & (
        count[:, :, None] > ids[None, None, :] % hold
    )
    rounds = (jnp.max(jnp.sum(all_to.astype(i32), axis=0)) + CAP - 1) // CAP

    own_holder = lax.dynamic_slice_in_dim(holder_of, me, 1, 0)[0]
    own_rank = lax.dynamic_slice_in_dim(rank, me, 1, 0)[0]
    page_rank = jnp.sum(
        jnp.where(own_holder[:, None] == ids[None, :], own_rank[None, :], 0), axis=1
    )
    page_nth = jnp.sum(
        (
            (page_ids[None, :] < page_ids[:, None])
            & (own_holder[None, :] == own_holder[:, None])
        ).astype(i32),
        axis=1,
    )
    unit = page_rank * hold + page_nth
    found = jnp.where(own_holder >= 0, (unit % holders) * places + unit // holders, 0)
    return pass_table, rounds, found


def staged(total, group, load, stage, packed, got_sem, put_sem):
    for g in range(total // group):
        for i in range(g * group, (g + 1) * group):
            load(i, got_sem.at[g])
    for g in range(total // group):
        part = pl.ds(g * group, group)
        pltpu.make_async_copy(stage.at[part], stage.at[part], got_sem.at[g]).wait()
        pltpu.make_async_copy(stage.at[part], packed.at[part], put_sem).start()
    pltpu.make_async_copy(stage, packed, put_sem).wait()


def pack_kernel(
    where_and_turn, page_table, keys, values, packed, table_v, table, stage, table_sem, got_sem, put_sem
):
    me, turn = where_and_turn[0], where_and_turn[1]
    requests, pages = page_table.shape
    slots = keys.shape[0]
    holders = packed.shape[0] // CAP
    groups = holders // HOLD
    i32 = jnp.int32
    slot_of = page_table[...]
    holder_of = jnp.where(slot_of >= 0, slot_of // slots, -1)
    local = slot_of % slots
    page_ids = lax.broadcasted_iota(i32, slot_of.shape, 1)
    mine = holder_of == me

    def first_of(on):
        return jnp.min(jnp.where(on, page_ids, pages), axis=1, keepdims=True)

    own_first = first_of(mine)
    rank = jnp.zeros((requests, 1), i32)
    for holder in range(holders):
        rank += (first_of(holder_of == holder) < own_first).astype(i32)
    mine_f = mine.astype(F32)
    count = jnp.sum(mine_f, axis=1, keepdims=True).astype(i32)
    before = lax.broadcasted_iota(i32, (pages, pages), 0) < lax.broadcasted_iota(
        i32, (pages, pages), 1
    )
    nth = jnp.dot(mine_f, before.astype(F32), preferred_element_type=F32).astype(i32)
    target = lax.broadcasted_iota(i32, (requests, holders), 1)
    to = (rank % groups == target // HOLD) & (count > target % HOLD)
    source = jnp.zeros((requests, holders), i32)
    for k in range(HOLD):
        hit = jnp.sum(jnp.where(mine & (nth == k), local, 0), axis=1, keepdims=True)
        source = jnp.where(target % HOLD == k, hit, source)
    earlier = lax.broadcasted_iota(i32, (requests, requests), 1) < lax.broadcasted_iota(
        i32, (requests, requests), 0
    )
    order = jnp.dot(
        earlier.astype(F32), to.astype(F32), preferred_element_type=F32
    ).astype(i32)
    for place in range(CAP):
        chosen = to & (order == turn * CAP + place)
        table_v[place : place + 1, 0:holders] = jnp.sum(
            jnp.where(chosen, source, 0), axis=0, keepdims=True
        )
    copy = pltpu.make_async_copy(table_v, table, table_sem)
    copy.start()
    copy.wait()

    def load(i, sem):
        slot = table[i % CAP, i // CAP]
        pltpu.make_async_copy(keys.at[slot], stage.at[i, 0], sem).start()
        pltpu.make_async_copy(values.at[slot], stage.at[i, 1], sem).start()

    staged(stage.shape[0], GROUP, load, stage, packed, got_sem, put_sem)


def repack_kernel(table, got, packed, stage, got_sem, put_sem):
    def load(i, sem):
        pltpu.make_async_copy(got.at[jnp.maximum(table[i], 0)], stage.at[i], sem).start()

    staged(stage.shape[0], GROUP, load, stage, packed, got_sem, put_sem)


def staging(shape):
    return [
        pltpu.VMEM(shape, BF16),
        pltpu.SemaphoreType.DMA((shape[0] // GROUP,)),
        pltpu.SemaphoreType.DMA,
    ]


def pack_pages(me, turn, page_table, keys, values):
    shape = (lax.axis_size("pages") * CAP, 2) + keys.shape[1:]
    return pl.pallas_call(
        pack_kernel,
        out_shape=jax.ShapeDtypeStruct(shape, BF16),
        in_specs=[SMEM, VMEM, ANY, ANY],
        out_specs=ANY,
        scratch_shapes=[
            pltpu.VMEM((8, 128), jnp.int32),
            pltpu.SMEM((8, 128), jnp.int32),
            staging(shape)[0],
            pltpu.SemaphoreType.DMA,
        ]
        + staging(shape)[1:],
        compiler_params=pltpu.CompilerParams(vmem_limit_bytes=60 << 20),
        name="pack_pages",
    )(jnp.stack([me, turn]).astype(jnp.int32), page_table, keys, values)


def repack_pages(table, got):
    return pl.pallas_call(
        repack_kernel,
        out_shape=jax.ShapeDtypeStruct(got.shape, BF16),
        in_specs=[SMEM, ANY],
        out_specs=ANY,
        scratch_shapes=staging(got.shape),
        compiler_params=pltpu.CompilerParams(vmem_limit_bytes=60 << 20),
        name="repack_pages",
    )(table, got)


def exchange(pages):
    holders = lax.axis_size("pages")
    shape = pages.shape
    sent = lax.all_to_all(
        pages.reshape((holders, shape[0] // holders) + shape[1:]), "pages", 0, 0, tiled=True
    )
    return sent.reshape(shape)


def pages_to_owners(page_table, keys, values, later):
    holders = lax.axis_size("pages")
    me = lax.axis_index("pages")
    packed, table, later = lax.optimization_barrier(
        (pack_pages(me, 0, page_table, keys, values), page_table, later)
    )
    pass_table, rounds, found = routing(table, me, holders, keys.shape[0], HOLD)
    x_parts = lax.all_gather(later[0], "mlp", axis=0)
    first, x_parts = lax.optimization_barrier((exchange(packed), x_parts))
    middle = repack_pages(pass_table(0), first)

    def further(turn, middle):
        got = exchange(pack_pages(me, turn, page_table, keys, values))
        table = pass_table(turn)
        return jnp.where((table >= 0)[:, None, None, None], repack_pages(table, got), middle)

    middle = lax.fori_loop(1, rounds, further, middle)
    return exchange(middle), found, x_parts, later[1:]


def two_heads(rows):
    lane = lax.broadcasted_iota(jnp.int32, rows.shape, 1)
    low = jnp.where(lane < HD, rows, 0.0)
    high = jnp.where(lane < HD, 0.0, rows)
    return jnp.concatenate([low, high], axis=0).astype(BF16)


def project_kernel(x_ref, wq, wk, wv, wg, queries, global_rows, key_rows, value_rows, x_all):
    shards, _, width = x_ref.shape
    for i in range(shards):
        x_all[:, i * width : (i + 1) * width] = x_ref[i]
    x = x_all[...]

    def project(matrix):
        return jnp.dot(x, matrix[...], preferred_element_type=F32).astype(BF16)

    scale = HD ** (-0.5)
    queries[...] = two_heads(project(wq).astype(F32) * scale)
    global_rows[...] = two_heads(project(wg).astype(F32) * scale)
    key_rows[...] = project(wk)
    value_rows[...] = project(wv)


def project_all(x_parts, wq, wk, wv, wg):
    shards, rows, width = x_parts.shape
    doubled = jax.ShapeDtypeStruct((2 * rows, width), BF16)
    single = jax.ShapeDtypeStruct((rows, width), BF16)
    return pl.pallas_call(
        project_kernel,
        out_shape=(doubled, doubled, single, single),
        in_specs=[VMEM] * 5,
        out_specs=(VMEM,) * 4,
        scratch_shapes=[pltpu.VMEM((rows, shards * width), BF16)],
        name="project",
    )(x_parts, wq, wk, wv, wg)


def attention_kernel(inner, found, length, *refs):
    given = refs[: 5 if inner else 4]
    pages, out, key_buf, value_buf, kept, peak, acc, ksem, vsem = refs[len(given) :][:9]
    projected = refs[len(given) + 9 :]
    queries, global_rows, key_rows, value_rows = projected[:4] if inner else given
    per_block = KEY_BLOCK // PAGE
    shards, rows, width = out.shape
    limit = length[0]
    blocks = (limit + KEY_BLOCK - 1) // KEY_BLOCK

    def block_rows(block):
        return pl.ds(pl.multiple_of(block * KEY_BLOCK, KEY_BLOCK), KEY_BLOCK)

    def fetch(block, carry, part, buf, sem):
        for i in range(per_block):
            page = block * per_block + i
            rows = pl.ds(pl.multiple_of(page * PAGE, PAGE), PAGE)
            pltpu.make_async_copy(pages.at[found[page], part], buf.at[rows], sem.at[block]).start()
        return carry

    lax.fori_loop(0, blocks, functools.partial(fetch, part=0, buf=key_buf, sem=ksem), 0)
    lax.fori_loop(0, blocks, functools.partial(fetch, part=1, buf=value_buf, sem=vsem), 0)
    if inner:
        project_kernel(*given, *projected)
    def scores_of(left, keys):
        return lax.dot_general(
            left, keys, (((1,), (1,)), ((), ())), preferred_element_type=F32
        ) * LOG2E

    def fold(scores):
        parts = [scores[:, i : i + 128] for i in range(0, scores.shape[1], 128)]
        while len(parts) > 1:
            parts = [jnp.maximum(*parts[i : i + 2]) for i in range(0, len(parts), 2)]
        return parts[0]

    def weigh(scores, top, values):
        ones = jnp.ones(values.shape, BF16)
        weights = jnp.exp2(scores - top).astype(BF16)
        return jnp.dot(
            weights, jnp.concatenate([values, ones], axis=1), preferred_element_type=F32
        )

    own = scores_of(queries[...], key_rows[...])
    peak[...] = fold(own)

    def score_step(block, carry):
        part = key_buf.at[block_rows(block)]
        pltpu.make_async_copy(part, part, ksem.at[block]).wait()
        scores = scores_of(global_rows[...], key_buf[block_rows(block), :])
        position = block * KEY_BLOCK + lax.broadcasted_iota(jnp.int32, scores.shape, 1)
        scores = jnp.where(position < limit, scores, NEG)
        kept[block] = scores
        peak[...] = jnp.maximum(peak[...], fold(scores))
        return carry

    lax.fori_loop(0, blocks, score_step, 0)
    top = jnp.max(peak[...], axis=1, keepdims=True)
    peak[...] = jnp.broadcast_to(top, peak.shape)
    acc[...] = weigh(own, top, value_rows[...])

    def weigh_step(block, carry):
        part = value_buf.at[block_rows(block)]
        pltpu.make_async_copy(part, part, vsem.at[block]).wait()
        acc[...] += weigh(kept[block], peak[:, :1], value_buf[block_rows(block), :])
        return carry

    lax.fori_loop(0, blocks, weigh_step, 0)
    total = acc[...]
    ratio = total[:, :width] / total[:, width:]
    lane = lax.broadcasted_iota(jnp.int32, (rows, width), 1)
    result = jnp.where(lane < HD, ratio[:rows], ratio[rows:]).astype(BF16)
    for i in range(shards):
        out[i] = result


def attend(found, length, shards, given, pages):
    inner = len(given) == 5
    rows, width = given[0].shape[1:] if inner else given[2].shape
    longest = found.shape[0] * PAGE
    scratch = [
        pltpu.VMEM((longest, width), BF16),
        pltpu.VMEM((longest, width), BF16),
        pltpu.VMEM((longest // KEY_BLOCK, 2 * rows, KEY_BLOCK), F32),
        pltpu.VMEM((2 * rows, 128), F32),
        pltpu.VMEM((2 * rows, 2 * width), F32),
        pltpu.SemaphoreType.DMA((longest // KEY_BLOCK,)),
        pltpu.SemaphoreType.DMA((longest // KEY_BLOCK,)),
    ]
    if inner:
        scratch += [
            pltpu.VMEM((2 * rows, width), BF16),
            pltpu.VMEM((2 * rows, width), BF16),
            pltpu.VMEM((rows, width), BF16),
            pltpu.VMEM((rows, width), BF16),
            pltpu.VMEM((rows, shards * width), BF16),
        ]
    return pl.pallas_call(
        functools.partial(attention_kernel, inner),
        out_shape=jax.ShapeDtypeStruct((shards, rows, width), BF16),
        in_specs=[SMEM, SMEM] + [VMEM] * len(given) + [ANY],
        out_specs=VMEM,
        scratch_shapes=scratch,
        compiler_params=pltpu.CompilerParams(vmem_limit_bytes=(50 if inner else 56) << 20),
        name="attention",
    )(found, length, *given, pages)


def normalize(total, gain, bias, width):
    mean = jnp.sum(total, axis=1, keepdims=True) * (1.0 / width)
    square = jnp.sum(total * total, axis=1, keepdims=True) * (1.0 / width)
    inverse = lax.rsqrt(square - mean * mean + EPS)
    return ((total - mean) * inverse * gain + bias).astype(BF16)


def ffn_kernel(
    column,
    att,
    x_ref,
    accept,
    w_out,
    up_a,
    up_b,
    down_a,
    down_b,
    g1,
    b1,
    g2,
    b2,
    out,
    wide,
    hidden,
    acc,
):
    step = pl.program_id(0)
    shards, rows, width = x_ref.shape
    full = shards * width

    @pl.when(step == 0)
    def _():
        for i in range(shards):
            wide[:, i * width : (i + 1) * width] = att[i]
        total = jnp.dot(wide[...], w_out[...], preferred_element_type=F32)
        for i in range(shards):
            wide[:, i * width : (i + 1) * width] = x_ref[i]
        total = total + wide[...].astype(F32)
        hidden[...] = normalize(total, g1[...], b1[...], full)
        acc[...] = hidden[...].astype(F32)

    h = hidden[...]
    raised = [
        jnp.dot(h, up[i], preferred_element_type=F32)
        for i in range(up_a.shape[0])
        for up in (up_a, up_b)
    ]
    active = [(0.5 * v * (1.0 + lax.erf(v * (0.5**0.5)))).astype(BF16) for v in raised]
    downs = [down[i] for i in range(up_a.shape[0]) for down in (down_a, down_b)]
    acc[...] += jnp.dot(
        jnp.concatenate(active, axis=1),
        jnp.concatenate(downs, axis=0),
        preferred_element_type=F32,
    )

    @pl.when(step == pl.num_programs(0) - 1)
    def _():
        result = normalize(acc[...], g2[...], b2[...], full)
        chosen = accept[...] != 0
        if out.shape[0] == shards:
            for i in range(shards):
                out[i] = jnp.where(chosen, result[:, i * width : (i + 1) * width], x_ref[i])
        else:
            for i in range(shards):

                @pl.when(column[0] == i)
                def _():
                    out[0] = jnp.where(chosen, result[:, i * width : (i + 1) * width], x_ref[i])


def feed_forward(column, outs, att, x_parts, accept, w_out, up, down, g1, b1, g2, b2):
    shards, rows, width = x_parts.shape
    full = shards * width
    units = up[0].shape[2]

    def fixed(shape):
        return pl.BlockSpec(shape, lambda i: (0,) * len(shape), pipeline_mode=pl.Buffered(1))

    def part(*shape):
        return pl.BlockSpec((PER,) + shape, lambda i: (i, 0, 0))

    return pl.pallas_call(
        ffn_kernel,
        grid=(shards // PER,),
        out_shape=jax.ShapeDtypeStruct((outs, rows, width), BF16),
        in_specs=[SMEM, fixed(x_parts.shape), fixed(x_parts.shape), fixed((rows, 1))]
        + [fixed(w_out.shape)]
        + [part(full, units)] * 2
        + [part(units, full)] * 2
        + [fixed((1, full))] * 4,
        out_specs=pl.BlockSpec((outs, rows, width), lambda i: (0, 0, 0)),
        scratch_shapes=[
            pltpu.VMEM((rows, full), BF16),
            pltpu.VMEM((rows, full), BF16),
            pltpu.VMEM((rows, full), F32),
        ],
        compiler_params=pltpu.CompilerParams(
            dimension_semantics=("arbitrary",), vmem_limit_bytes=52 << 20
        ),
        name="feed_forward",
    )(column, att, x_parts, accept, w_out, *up, *down, g1, b1, g2, b2)


def to_all(copies):
    return lax.all_to_all(copies, "mlp", 0, 0, tiled=True)


def core_pair():
    return [(i, i ^ 1) for i in range(lax.axis_size("pages"))]


def per_device(
    embeddings,
    w_query,
    w_key,
    w_value,
    w_global_query,
    w_out,
    w_up,
    w_down,
    norm1_gain,
    norm1_bias,
    norm2_gain,
    norm2_bias,
    cache_keys,
    cache_values,
    lengths,
    page_table,
    accept,
):
    shards = lax.axis_size("mlp")
    me = lax.axis_index("pages")
    shard = lax.axis_index("mlp")
    rows, width = embeddings.shape
    core = me % 2
    half_out = w_out.shape[0] // 2
    out_half = lax.dynamic_slice_in_dim(w_out, core * half_out, half_out, 0)
    out_mine = lax.all_gather(out_half, "mlp", axis=0)
    pages, found, x_parts, (w_up, w_down) = pages_to_owners(
        page_table, cache_keys, cache_values, (embeddings, w_up, w_down)
    )
    length = lax.dynamic_slice_in_dim(lengths, me, 1, 0)

    half = w_up.shape[1] // 2
    up_half = lax.dynamic_slice_in_dim(w_up, core * half, half, 1)
    down_half = lax.dynamic_slice_in_dim(w_down, core * half, half, 0)
    up_mine = lax.all_gather(up_half, "mlp", axis=0)
    down_mine = lax.all_gather(down_half, "mlp", axis=0)
    norms = [v.reshape(1, -1) for v in (norm1_gain, norm1_bias, norm2_gain, norm2_bias)]
    column = shard.reshape(1).astype(jnp.int32)
    projections = (w_query, w_key, w_value, w_global_query)

    def swap(array):
        return lax.ppermute(array, "pages", core_pair())

    out_other = swap(out_mine)
    w_out_all = jnp.where(
        core == 0, jnp.stack([out_mine, out_other], 1), jnp.stack([out_other, out_mine], 1)
    ).reshape(shards * w_out.shape[0], -1)
    up = (up_mine, swap(up_mine))
    pages, up, w_out_all = lax.optimization_barrier((pages, up, w_out_all))

    def layer(outs, attention, x_parts, taken, down):
        return feed_forward(
            column,
            outs,
            to_all(attention),
            x_parts,
            taken.reshape(rows, 1),
            w_out_all,
            up,
            down,
            *norms,
        )

    attention = attend(found, length, shards, project_all(x_parts, *projections), pages)
    attention, down_mine = lax.optimization_barrier((attention, down_mine))
    down = (down_mine, swap(down_mine))
    middle = layer(shards, attention, x_parts, accept[0], down)
    attention = attend(found, length, shards, (middle,) + projections, pages)
    return layer(1, attention, middle, accept[1], down).reshape(rows, width)


def solution(mesh):
    return jax.shard_map(
        per_device,
        mesh=mesh,
        in_specs=(
            P("pages", "mlp"),
            P(None, "mlp"),
            P(None, "mlp"),
            P(None, "mlp"),
            P(None, "mlp"),
            P("mlp", None),
            P(None, "mlp"),
            P("mlp", None),
            P(),
            P(),
            P(),
            P(),
            P("pages", None, "mlp"),
            P("pages", None, "mlp"),
            P(),
            P(),
            P(None, "pages"),
        ),
        out_specs=P("pages", "mlp"),
        check_vma=False,
    )
```

```python
import functools

import jax
import jax.numpy as jnp
from jax import lax
from jax.experimental import pallas as pl
from jax.experimental.pallas import tpu as pltpu
from jax.sharding import PartitionSpec as P

HD = 64
BLK = 256
PAGE = 128
EPS = 1e-05
NEG = -1e30
CAP = 2
KEY_BLOCK = 4096
GROUP = 8
HOLD = 8
PER = 2
LOG2E = 1.4426950408889634
F32 = jnp.float32
BF16 = jnp.bfloat16
VMEM = pl.BlockSpec(memory_space=pltpu.VMEM)
ANY = pl.BlockSpec(memory_space=pl.ANY)
SMEM = pl.BlockSpec(memory_space=pltpu.SMEM)


def routing(page_table, me, holders, slots, hold):
    requests, pages = page_table.shape
    i32 = jnp.int32
    holder_of = jnp.where(page_table >= 0, page_table // slots, -1)
    ids = jnp.arange(holders, dtype=i32)
    page_ids = jnp.arange(pages, dtype=i32)
    on = holder_of[:, None, :] == ids[None, :, None]
    first = jnp.min(jnp.where(on, page_ids[None, None, :], pages), axis=2)
    count = jnp.sum(on.astype(i32), axis=2)
    rank = jnp.sum((first[:, None, :] < first[:, :, None]).astype(i32), axis=2)
    groups = holders // hold
    request_ids = jnp.arange(requests, dtype=i32)
    earlier = request_ids[None, :] < request_ids[:, None]

    def before(sent):
        return jnp.sum((earlier[:, :, None] & sent[None, :, :]).astype(i32), axis=1)

    places = pages // holders
    came = (rank % groups == me // hold) & (count > me % hold)
    came_turn = before(came)

    def pass_table(turn):
        place = rank // groups
        chosen = (
            came[:, :, None]
            & (place[:, :, None] == jnp.arange(places, dtype=i32)[None, None, :])
            & (came_turn // CAP == turn)[:, :, None]
        )
        origin = ids[None, :] * CAP + came_turn % CAP + 1
        return (jnp.sum(jnp.where(chosen, origin[:, :, None], 0), axis=1) - 1).reshape(-1)

    all_to = (rank[:, :, None] % groups == ids[None, None, :] // hold) & (
        count[:, :, None] > ids[None, None, :] % hold
    )
    rounds = (jnp.max(jnp.sum(all_to.astype(i32), axis=0)) + CAP - 1) // CAP

    own_holder = lax.dynamic_slice_in_dim(holder_of, me, 1, 0)[0]
    own_rank = lax.dynamic_slice_in_dim(rank, me, 1, 0)[0]
    page_rank = jnp.sum(
        jnp.where(own_holder[:, None] == ids[None, :], own_rank[None, :], 0), axis=1
    )
    page_nth = jnp.sum(
        (
            (page_ids[None, :] < page_ids[:, None])
            & (own_holder[None, :] == own_holder[:, None])
        ).astype(i32),
        axis=1,
    )
    unit = page_rank * hold + page_nth
    found = jnp.where(own_holder >= 0, (unit % holders) * places + unit // holders, 0)
    return pass_table, rounds, found


def staged(total, group, load, stage, packed, got_sem, put_sem):
    for g in range(total // group):
        for i in range(g * group, (g + 1) * group):
            load(i, got_sem.at[g])
    for g in range(total // group):
        part = pl.ds(g * group, group)
        pltpu.make_async_copy(stage.at[part], stage.at[part], got_sem.at[g]).wait()
        pltpu.make_async_copy(stage.at[part], packed.at[part], put_sem).start()
    pltpu.make_async_copy(stage, packed, put_sem).wait()


def pack_kernel(
    where_and_turn, page_table, keys, values, packed, table_v, table, stage, table_sem, got_sem, put_sem
):
    me, turn = where_and_turn[0], where_and_turn[1]
    requests, pages = page_table.shape
    slots = keys.shape[0]
    holders = packed.shape[0] // CAP
    groups = holders // HOLD
    i32 = jnp.int32
    slot_of = page_table[...]
    holder_of = jnp.where(slot_of >= 0, slot_of // slots, -1)
    local = slot_of % slots
    page_ids = lax.broadcasted_iota(i32, slot_of.shape, 1)
    mine = holder_of == me

    def first_of(on):
        return jnp.min(jnp.where(on, page_ids, pages), axis=1, keepdims=True)

    own_first = first_of(mine)
    rank = jnp.zeros((requests, 1), i32)
    for holder in range(holders):
        rank += (first_of(holder_of == holder) < own_first).astype(i32)
    mine_f = mine.astype(F32)
    count = jnp.sum(mine_f, axis=1, keepdims=True).astype(i32)
    before = lax.broadcasted_iota(i32, (pages, pages), 0) < lax.broadcasted_iota(
        i32, (pages, pages), 1
    )
    nth = jnp.dot(mine_f, before.astype(F32), preferred_element_type=F32).astype(i32)
    target = lax.broadcasted_iota(i32, (requests, holders), 1)
    to = (rank % groups == target // HOLD) & (count > target % HOLD)
    source = jnp.zeros((requests, holders), i32)
    for k in range(HOLD):
        hit = jnp.sum(jnp.where(mine & (nth == k), local, 0), axis=1, keepdims=True)
        source = jnp.where(target % HOLD == k, hit, source)
    earlier = lax.broadcasted_iota(i32, (requests, requests), 1) < lax.broadcasted_iota(
        i32, (requests, requests), 0
    )
    order = jnp.dot(
        earlier.astype(F32), to.astype(F32), preferred_element_type=F32
    ).astype(i32)
    for place in range(CAP):
        chosen = to & (order == turn * CAP + place)
        table_v[place : place + 1, 0:holders] = jnp.sum(
            jnp.where(chosen, source, 0), axis=0, keepdims=True
        )
    copy = pltpu.make_async_copy(table_v, table, table_sem)
    copy.start()
    copy.wait()

    def load(i, sem):
        slot = table[i % CAP, i // CAP]
        pltpu.make_async_copy(keys.at[slot], stage.at[i, 0], sem).start()
        pltpu.make_async_copy(values.at[slot], stage.at[i, 1], sem).start()

    staged(stage.shape[0], GROUP, load, stage, packed, got_sem, put_sem)


def repack_kernel(table, got, packed, stage, got_sem, put_sem):
    def load(i, sem):
        pltpu.make_async_copy(got.at[jnp.maximum(table[i], 0)], stage.at[i], sem).start()

    staged(stage.shape[0], GROUP, load, stage, packed, got_sem, put_sem)


def staging(shape):
    return [
        pltpu.VMEM(shape, BF16),
        pltpu.SemaphoreType.DMA((shape[0] // GROUP,)),
        pltpu.SemaphoreType.DMA,
    ]


def pack_pages(me, turn, page_table, keys, values):
    shape = (lax.axis_size("pages") * CAP, 2) + keys.shape[1:]
    return pl.pallas_call(
        pack_kernel,
        out_shape=jax.ShapeDtypeStruct(shape, BF16),
        in_specs=[SMEM, VMEM, ANY, ANY],
        out_specs=ANY,
        scratch_shapes=[
            pltpu.VMEM((8, 128), jnp.int32),
            pltpu.SMEM((8, 128), jnp.int32),
            staging(shape)[0],
            pltpu.SemaphoreType.DMA,
        ]
        + staging(shape)[1:],
        compiler_params=pltpu.CompilerParams(vmem_limit_bytes=60 << 20),
        name="pack_pages",
    )(jnp.stack([me, turn]).astype(jnp.int32), page_table, keys, values)


def repack_pages(table, got):
    return pl.pallas_call(
        repack_kernel,
        out_shape=jax.ShapeDtypeStruct(got.shape, BF16),
        in_specs=[SMEM, ANY],
        out_specs=ANY,
        scratch_shapes=staging(got.shape),
        compiler_params=pltpu.CompilerParams(vmem_limit_bytes=60 << 20),
        name="repack_pages",
    )(table, got)


def exchange(pages):
    holders = lax.axis_size("pages")
    shape = pages.shape
    sent = lax.all_to_all(
        pages.reshape((holders, shape[0] // holders) + shape[1:]), "pages", 0, 0, tiled=True
    )
    return sent.reshape(shape)


def pages_to_owners(page_table, keys, values, later):
    holders = lax.axis_size("pages")
    me = lax.axis_index("pages")
    packed, table, later = lax.optimization_barrier(
        (pack_pages(me, 0, page_table, keys, values), page_table, later)
    )
    pass_table, rounds, found = routing(table, me, holders, keys.shape[0], HOLD)
    x_parts = lax.all_gather(later[0], "mlp", axis=0)
    first, x_parts = lax.optimization_barrier((exchange(packed), x_parts))
    middle = repack_pages(pass_table(0), first)

    def further(turn, middle):
        got = exchange(pack_pages(me, turn, page_table, keys, values))
        table = pass_table(turn)
        return jnp.where((table >= 0)[:, None, None, None], repack_pages(table, got), middle)

    middle = lax.fori_loop(1, rounds, further, middle)
    return exchange(middle), found, x_parts, later[1:]


def two_heads(rows):
    lane = lax.broadcasted_iota(jnp.int32, rows.shape, 1)
    low = jnp.where(lane < HD, rows, 0.0)
    high = jnp.where(lane < HD, 0.0, rows)
    return jnp.concatenate([low, high], axis=0).astype(BF16)


def project_kernel(x_ref, wq, wk, wv, wg, queries, global_rows, key_rows, value_rows, x_all):
    shards, _, width = x_ref.shape
    for i in range(shards):
        x_all[:, i * width : (i + 1) * width] = x_ref[i]
    x = x_all[...]

    def project(matrix):
        return jnp.dot(x, matrix[...], preferred_element_type=F32).astype(BF16)

    scale = HD ** (-0.5)
    queries[...] = two_heads(project(wq).astype(F32) * scale)
    global_rows[...] = two_heads(project(wg).astype(F32) * scale)
    key_rows[...] = project(wk)
    value_rows[...] = project(wv)


def project_all(x_parts, wq, wk, wv, wg):
    shards, rows, width = x_parts.shape
    doubled = jax.ShapeDtypeStruct((2 * rows, width), BF16)
    single = jax.ShapeDtypeStruct((rows, width), BF16)
    return pl.pallas_call(
        project_kernel,
        out_shape=(doubled, doubled, single, single),
        in_specs=[VMEM] * 5,
        out_specs=(VMEM,) * 4,
        scratch_shapes=[pltpu.VMEM((rows, shards * width), BF16)],
        name="project",
    )(x_parts, wq, wk, wv, wg)


def attention_kernel(inner, found, length, *refs):
    given = refs[: 5 if inner else 4]
    pages, out, key_buf, value_buf, kept, peak, acc, ksem, vsem = refs[len(given) :][:9]
    projected = refs[len(given) + 9 :]
    queries, global_rows, key_rows, value_rows = projected[:4] if inner else given
    per_block = KEY_BLOCK // PAGE
    shards, rows, width = out.shape
    limit = length[0]
    blocks = (limit + KEY_BLOCK - 1) // KEY_BLOCK

    def block_rows(block):
        return pl.ds(pl.multiple_of(block * KEY_BLOCK, KEY_BLOCK), KEY_BLOCK)

    def fetch(block, carry, part, buf, sem):
        for i in range(per_block):
            page = block * per_block + i
            rows = pl.ds(pl.multiple_of(page * PAGE, PAGE), PAGE)
            pltpu.make_async_copy(pages.at[found[page], part], buf.at[rows], sem.at[block]).start()
        return carry

    lax.fori_loop(0, blocks, functools.partial(fetch, part=0, buf=key_buf, sem=ksem), 0)
    lax.fori_loop(0, blocks, functools.partial(fetch, part=1, buf=value_buf, sem=vsem), 0)
    if inner:
        project_kernel(*given, *projected)
    def scores_of(left, keys):
        return lax.dot_general(
            left, keys, (((1,), (1,)), ((), ())), preferred_element_type=F32
        ) * LOG2E

    def fold(scores):
        parts = [scores[:, i : i + 128] for i in range(0, scores.shape[1], 128)]
        while len(parts) > 1:
            parts = [jnp.maximum(*parts[i : i + 2]) for i in range(0, len(parts), 2)]
        return parts[0]

    def weigh(scores, top, values):
        ones = jnp.ones(values.shape, BF16)
        weights = jnp.exp2(scores - top).astype(BF16)
        return jnp.dot(
            weights, jnp.concatenate([values, ones], axis=1), preferred_element_type=F32
        )

    own = scores_of(queries[...], key_rows[...])
    peak[...] = fold(own)

    def score_step(block, carry):
        part = key_buf.at[block_rows(block)]
        pltpu.make_async_copy(part, part, ksem.at[block]).wait()
        scores = scores_of(global_rows[...], key_buf[block_rows(block), :])
        position = block * KEY_BLOCK + lax.broadcasted_iota(jnp.int32, scores.shape, 1)
        scores = jnp.where(position < limit, scores, NEG)
        kept[block] = scores
        peak[...] = jnp.maximum(peak[...], fold(scores))
        return carry

    lax.fori_loop(0, blocks, score_step, 0)
    top = jnp.max(peak[...], axis=1, keepdims=True)
    peak[...] = jnp.broadcast_to(top, peak.shape)
    acc[...] = weigh(own, top, value_rows[...])

    def weigh_step(block, carry):
        part = value_buf.at[block_rows(block)]
        pltpu.make_async_copy(part, part, vsem.at[block]).wait()
        acc[...] += weigh(kept[block], peak[:, :1], value_buf[block_rows(block), :])
        return carry

    lax.fori_loop(0, blocks, weigh_step, 0)
    total = acc[...]
    ratio = total[:, :width] / total[:, width:]
    lane = lax.broadcasted_iota(jnp.int32, (rows, width), 1)
    result = jnp.where(lane < HD, ratio[:rows], ratio[rows:]).astype(BF16)
    for i in range(shards):
        out[i] = result


def attend(found, length, shards, given, pages):
    inner = len(given) == 5
    rows, width = given[0].shape[1:] if inner else given[2].shape
    longest = found.shape[0] * PAGE
    scratch = [
        pltpu.VMEM((longest, width), BF16),
        pltpu.VMEM((longest, width), BF16),
        pltpu.VMEM((longest // KEY_BLOCK, 2 * rows, KEY_BLOCK), F32),
        pltpu.VMEM((2 * rows, 128), F32),
        pltpu.VMEM((2 * rows, 2 * width), F32),
        pltpu.SemaphoreType.DMA((longest // KEY_BLOCK,)),
        pltpu.SemaphoreType.DMA((longest // KEY_BLOCK,)),
    ]
    if inner:
        scratch += [
            pltpu.VMEM((2 * rows, width), BF16),
            pltpu.VMEM((2 * rows, width), BF16),
            pltpu.VMEM((rows, width), BF16),
            pltpu.VMEM((rows, width), BF16),
            pltpu.VMEM((rows, shards * width), BF16),
        ]
    return pl.pallas_call(
        functools.partial(attention_kernel, inner),
        out_shape=jax.ShapeDtypeStruct((shards, rows, width), BF16),
        in_specs=[SMEM, SMEM] + [VMEM] * len(given) + [ANY],
        out_specs=VMEM,
        scratch_shapes=scratch,
        compiler_params=pltpu.CompilerParams(vmem_limit_bytes=(50 if inner else 56) << 20),
        name="attention",
    )(found, length, *given, pages)


def normalize(total, gain, bias, width):
    mean = jnp.sum(total, axis=1, keepdims=True) * (1.0 / width)
    square = jnp.sum(total * total, axis=1, keepdims=True) * (1.0 / width)
    inverse = lax.rsqrt(square - mean * mean + EPS)
    return ((total - mean) * inverse * gain + bias).astype(BF16)


def ffn_kernel(
    column,
    att,
    x_ref,
    accept,
    w_out,
    up_a,
    up_b,
    down_a,
    down_b,
    g1,
    b1,
    g2,
    b2,
    out,
    wide,
    hidden,
    acc,
):
    step = pl.program_id(0)
    shards, rows, width = x_ref.shape
    full = shards * width

    @pl.when(step == 0)
    def _():
        for i in range(shards):
            wide[:, i * width : (i + 1) * width] = att[i]
        total = jnp.dot(wide[...], w_out[...], preferred_element_type=F32)
        for i in range(shards):
            wide[:, i * width : (i + 1) * width] = x_ref[i]
        total = total + wide[...].astype(F32)
        hidden[...] = normalize(total, g1[...], b1[...], full)
        acc[...] = hidden[...].astype(F32)

    h = hidden[...]
    raised = [
        jnp.dot(h, up[i], preferred_element_type=F32)
        for i in range(up_a.shape[0])
        for up in (up_a, up_b)
    ]
    active = [(0.5 * v * (1.0 + lax.erf(v * (0.5**0.5)))).astype(BF16) for v in raised]
    downs = [down[i] for i in range(up_a.shape[0]) for down in (down_a, down_b)]
    acc[...] += jnp.dot(
        jnp.concatenate(active, axis=1),
        jnp.concatenate(downs, axis=0),
        preferred_element_type=F32,
    )

    @pl.when(step == pl.num_programs(0) - 1)
    def _():
        result = normalize(acc[...], g2[...], b2[...], full)
        chosen = accept[...] != 0
        if out.shape[0] == shards:
            for i in range(shards):
                out[i] = jnp.where(chosen, result[:, i * width : (i + 1) * width], x_ref[i])
        else:
            for i in range(shards):

                @pl.when(column[0] == i)
                def _():
                    out[0] = jnp.where(chosen, result[:, i * width : (i + 1) * width], x_ref[i])


def feed_forward(column, outs, att, x_parts, accept, w_out, up, down, g1, b1, g2, b2):
    shards, rows, width = x_parts.shape
    full = shards * width
    units = up[0].shape[2]

    def fixed(shape):
        return pl.BlockSpec(shape, lambda i: (0,) * len(shape), pipeline_mode=pl.Buffered(1))

    def part(*shape):
        return pl.BlockSpec((PER,) + shape, lambda i: (i, 0, 0))

    return pl.pallas_call(
        ffn_kernel,
        grid=(shards // PER,),
        out_shape=jax.ShapeDtypeStruct((outs, rows, width), BF16),
        in_specs=[SMEM, fixed(x_parts.shape), fixed(x_parts.shape), fixed((rows, 1))]
        + [fixed(w_out.shape)]
        + [part(full, units)] * 2
        + [part(units, full)] * 2
        + [fixed((1, full))] * 4,
        out_specs=pl.BlockSpec((outs, rows, width), lambda i: (0, 0, 0)),
        scratch_shapes=[
            pltpu.VMEM((rows, full), BF16),
            pltpu.VMEM((rows, full), BF16),
            pltpu.VMEM((rows, full), F32),
        ],
        compiler_params=pltpu.CompilerParams(
            dimension_semantics=("arbitrary",), vmem_limit_bytes=52 << 20
        ),
        name="feed_forward",
    )(column, att, x_parts, accept, w_out, *up, *down, g1, b1, g2, b2)


def to_all(copies):
    return lax.all_to_all(copies, "mlp", 0, 0, tiled=True)


def core_pair():
    return [(i, i ^ 1) for i in range(lax.axis_size("pages"))]


def per_device(
    embeddings,
    w_query,
    w_key,
    w_value,
    w_global_query,
    w_out,
    w_up,
    w_down,
    norm1_gain,
    norm1_bias,
    norm2_gain,
    norm2_bias,
    cache_keys,
    cache_values,
    lengths,
    page_table,
    accept,
):
    shards = lax.axis_size("mlp")
    me = lax.axis_index("pages")
    shard = lax.axis_index("mlp")
    rows, width = embeddings.shape
    core = me % 2
    pages, found, x_parts, (w_up, w_down, w_out) = pages_to_owners(
        page_table, cache_keys, cache_values, (embeddings, w_up, w_down, w_out)
    )
    length = lax.dynamic_slice_in_dim(lengths, me, 1, 0)

    half = w_up.shape[1] // 2
    up_half = lax.dynamic_slice_in_dim(w_up, core * half, half, 1)
    down_half = lax.dynamic_slice_in_dim(w_down, core * half, half, 0)
    half_out = w_out.shape[0] // 2
    out_half = lax.dynamic_slice_in_dim(w_out, core * half_out, half_out, 0)
    blocks = w_out.shape[1] // half
    out_blocks = [out_half[:, i * half : (i + 1) * half] for i in range(blocks)]
    up_mine = lax.all_gather(jnp.concatenate([up_half] + out_blocks), "mlp", axis=0)
    down_mine = lax.all_gather(down_half, "mlp", axis=0)
    norms = [v.reshape(1, -1) for v in (norm1_gain, norm1_bias, norm2_gain, norm2_bias)]
    column = shard.reshape(1).astype(jnp.int32)
    projections = (w_query, w_key, w_value, w_global_query)

    def swap(array):
        return lax.ppermute(array, "pages", core_pair())

    up = (up_mine, swap(up_mine))

    def out_rows(array):
        tail = array[:, w_up.shape[0] :].reshape(shards, blocks, half_out, half)
        return jnp.swapaxes(tail, 1, 2).reshape(shards, half_out, w_out.shape[1])

    mine, other = out_rows(up[0]), out_rows(up[1])
    w_out_all = jnp.where(
        core == 0, jnp.stack([mine, other], 1), jnp.stack([other, mine], 1)
    ).reshape(shards * w_out.shape[0], w_out.shape[1])
    pages, up, w_out_all = lax.optimization_barrier((pages, up, w_out_all))

    def layer(outs, attention, x_parts, taken, down):
        return feed_forward(
            column,
            outs,
            to_all(attention),
            x_parts,
            taken.reshape(rows, 1),
            w_out_all,
            up,
            down,
            *norms,
        )

    attention = attend(found, length, shards, project_all(x_parts, *projections), pages)
    attention, down_mine = lax.optimization_barrier((attention, down_mine))
    down = (down_mine, swap(down_mine))
    middle = layer(shards, attention, x_parts, accept[0], down)
    attention = attend(found, length, shards, (middle,) + projections, pages)
    return layer(1, attention, middle, accept[1], down).reshape(rows, width)


def solution(mesh):
    return jax.shard_map(
        per_device,
        mesh=mesh,
        in_specs=(
            P("pages", "mlp"),
            P(None, "mlp"),
            P(None, "mlp"),
            P(None, "mlp"),
            P(None, "mlp"),
            P("mlp", None),
            P(None, "mlp"),
            P("mlp", None),
            P(),
            P(),
            P(),
            P(),
            P("pages", None, "mlp"),
            P("pages", None, "mlp"),
            P(),
            P(),
            P(None, "pages"),
        ),
        out_specs=P("pages", "mlp"),
        check_vma=False,
    )
```
